256 devices in a mesh: section: 8 (over y, x_lo), dev: 32 (over x_hi, z, core).
Axes of the slice: x: 4 (x_hi: 2, x_lo: 2; x = x_hi * 2 + x_lo), y: 4, z: 8, core: 2. Of those that a mesh axis runs over, the one named last changes fastest.
Arguments:
- patches: bfloat16 [8, 49152, 1280], P('section', 'dev'), may hold values from -6 to 6
- win_count: int32 [8, 32], P('section'), may hold values from 1 to 24, 256 in all within a row
- dest_perm: int32 [8, 32], P('section'), may hold values from 0 to 31, each once within a row
- win_groups: int32 [8, 32, 24], P('section'), may hold values from 2 to 16
- norm_gain: float32 [1280], replicated, may hold values from 0.5 to 1.5
- qkv_weight: bfloat16 [1280, 3840], P('dev')
- qkv_bias: float32 [3840], replicated, may hold values from -1.5 to 1.5
- proj_weight: bfloat16 [1280, 1280], P('dev'), may hold values from -0.15625 to 0.15625
- proj_bias: float32 [1280], replicated, may hold values from -1.5 to 1.5
- merge_gain: float32 [1280], replicated, may hold values from 0.5 to 1.5
- owner: int32 [8, 4096, 1], P('section', 'dev'), may hold values from 0 to 7; in each aligned block of 128 rows (0 to 127, 128 to 255, ..., all dimensions but the last counted through in order) at most 32 rows name the same one
Outputs:
- dispatched: bfloat16 [8, 8192, 5120], P('section', 'dev')
The draws below stay inside these ranges and needn't reach their ends.
Inputs may be any that keep to these rules, and one draw needn't show every extreme that they name: `win_count`: within each section's row the counts sum to 8 times the devices of dev, and the largest is 24. `dest_perm`: each section's row is a permutation. `win_groups`: entries of slots past a device's count are not read. Among the 128 rows of one device, at most 32 have the same owner, and some device of every draw reaches 32.
All inputs are finite; a program needn't handle non-finite values.
Results may differ from the reference program's by a relative error of at most 0.0051.
Values may be sent and summed in bfloat16 or wider, within the bound.
No kernel may reach another device: no remote copies, remote signals or barrier semaphores. Data moves between devices by JAX's collectives and lax.ppermute only.
A program may use at most 128 MiB of HBM per device.

```python
import math
import jax
import jax.numpy as jnp
import numpy as np
from jax import lax

D = 1280
HEADS = 16
HEAD_DIM = 80
WIN = 64
DST_WIN = 8
SRC_WIN = 24
MERGED = 128
CAP = 32
N_SECTION = 8
N_DEV = 32


def draw_qkv_weight(key, part):
    first = jax.random.fold_in(jax.random.fold_in(key, 11), 0)
    base = jax.random.normal(first, (D, 3 * D), jnp.float32) * D ** (-0.5)
    return base.astype(jnp.bfloat16)


def place_ends(array, rng, smallest, top_value):
    longest = array.shape.index(max(array.shape))
    spots = []
    for shift in (0, 1):
        where = [jax.random.randint(jax.random.fold_in(rng, axis), (), 0, length) for axis, length in enumerate(array.shape)]
        where[longest] = (where[longest] + shift) % array.shape[longest]
        spots.append(tuple(where))
    return array.at[spots[0]].set(smallest).at[spots[1]].set(top_value)


def block_levels(rng, dims, pieces, low, top_value):
    def one(position, parts):
        draws = jax.random.uniform(jax.random.fold_in(jax.random.fold_in(rng, 6), position), (parts,), jnp.float32, low / len(pieces), top_value / len(pieces))
        return jnp.repeat(jnp.exp(draws), dims[position] // parts).reshape((-1,) + (1,) * (len(dims) - position - 1))

    loudness = one(*pieces[0])
    for cut in pieces[1:]:
        loudness = loudness * one(*cut)
    return loudness


def profile(amount, total, most, lean):
    weights = [(1 << 20) // math.isqrt(rank ** lean) + 1 for rank in range(2, amount + 1)]
    surplus, given = total - most - (amount - 1), [1] * (amount - 1)
    while surplus > 0:
        free = [i for i in range(amount - 1) if given[i] < most]
        pool, budget = sum([weights[i] for i in free]), surplus
        for i in free:
            addition = min(most - given[i], max(1, budget * weights[i] // pool), surplus)
            given[i] = given[i] + addition
            surplus = surplus - addition
    return np.array([most] + given)


def ragged(rng, number_of, total, reach, lean):
    if number_of == 2:
        one = jax.random.randint(rng, (), max(1, total - reach), min(reach, total - 1) + 1)
        return jnp.stack([one, total - one])
    sizes = jnp.asarray(profile(number_of, total, reach, lean), jnp.int32)
    pairs = (number_of - 1) // 2
    donor, taker = sizes[1:1 + 2 * pairs:2], sizes[2:2 + 2 * pairs:2]
    room = jnp.minimum(donor - 1, reach - taker)
    passed = jax.random.randint(jax.random.fold_in(rng, 1), (pairs,), 0, 1 << 20) % (room + 1)
    sizes = sizes.at[1:1 + 2 * pairs:2].set(donor - passed).at[2:2 + 2 * pairs:2].set(taker + passed)
    return sizes[jax.random.permutation(jax.random.fold_in(rng, 2), number_of)]


def shared_out(rng, own, number, rows, count, top, limit, lean):
    sequence = jax.random.permutation(rng, count)
    packed, common = portions_of(count, rows * top, limit, lean, True), portions_of(count, rows * top, limit, lean, False)
    places = jnp.arange(count)

    def named(lengths, offset_by):
        used = int((lengths > 0).sum())
        fixed = max(1, used // 4)
        passed = fixed + (places - fixed + offset_by * (used - fixed)) % max(1, count - fixed)
        return jnp.zeros((count,), jnp.int32).at[sequence[jnp.where(places < fixed, places, passed)]].set(jnp.asarray(lengths, jnp.int32))

    lengths = jnp.where(number % 4 == 0, named(packed, number // 4), named(common, number - number // 4 - 1))
    mixed = jax.random.permutation(jax.random.fold_in(own, 3), count)
    donor, sink = mixed[0:count // 2 * 2:2], mixed[1:count // 2 * 2:2]
    room = jnp.minimum(lengths[donor] - 1, limit - lengths[sink]) // 2
    room = jnp.where((donor == sequence[0]) | (sink == sequence[0]) | (lengths[sink] == 0), 0, jnp.maximum(room, 0))
    passed = jax.random.randint(jax.random.fold_in(own, 4), (count // 2,), 0, 1 << 20) % (room + 1)
    lengths = lengths.at[donor].add(-passed).at[sink].add(passed)
    items = jnp.searchsorted(jnp.cumsum(lengths), jnp.arange(rows * top), side="right").astype(jnp.int32)
    listing = items.reshape(top, rows).T
    listing = listing[jax.random.permutation(jax.random.fold_in(own, 1), rows)]
    offset_by = jax.random.randint(jax.random.fold_in(own, 2), (rows, 1), 0, top)
    return jnp.take_along_axis(listing, (jnp.arange(top)[None, :] + offset_by) % top, axis=1)


def portions_of(count, total, most, skew, full):
    weights = [(1 << 20) // math.isqrt(grade ** skew) + 1 for grade in range(1, count + 1)]
    largest = most if full else min(most, max(-(-total // count), total * weights[0] // sum(weights)))
    least = 1 if total - largest >= count - 1 else 0
    holding, spare = [largest] + [least] * (count - 1), total - largest - least * (count - 1)
    while spare > 0:
        movable = [i for i in range(1, count) if holding[i] < largest] or [i for i in range(1, count) if holding[i] < most]
        mass, left = sum([weights[i] for i in movable]), spare
        for i in movable:
            more = min(most - holding[i], max(1, left * weights[i] // mass), spare)
            holding[i] = holding[i] + more
            spare = spare - more
    return np.array(holding)


def normal_values(own_key, dims, deviation, reach, pieces=(), kind=jnp.bfloat16):
    values = deviation * jax.random.normal(own_key, dims, jnp.float32)
    if pieces:
        values = values * block_levels(own_key, dims, pieces, -0.22, 0.18)
    return jnp.clip(values, -reach, reach).astype(kind)


def setup_inputs(seed: int = 0) -> dict:
    key_list = jax.random.split(jax.random.key(seed), 12)
    patches = normal_values(key_list[0], (N_SECTION, N_DEV * SRC_WIN * WIN, D), 1.0, 6.0, ((0, 8), (1, 32)))
    win_count = jax.vmap(lambda own: ragged(own, N_DEV, DST_WIN * N_DEV, SRC_WIN, 2))(jax.random.split(key_list[1], N_SECTION)).reshape((N_SECTION, N_DEV)).astype(jnp.int32)
    dest_perm = jax.vmap(lambda own: jax.random.permutation(own, N_DEV))(jax.random.split(key_list[2], N_SECTION)).reshape((N_SECTION, N_DEV)).astype(jnp.int32)
    win_groups = place_ends(jax.random.randint(key_list[3], (N_SECTION, N_DEV, SRC_WIN), 2, WIN // 4 + 1), jax.random.fold_in(key_list[3], 1), 2, (WIN // 4 + 1) - 1).astype(jnp.int32)
    norm_gain = jnp.clip(1.0 + 0.1 * jax.random.normal(key_list[4], (D,), jnp.float32), 0.5, 1.5)
    qkv_weight = draw_qkv_weight(jax.random.fold_in(key_list[11], 71), 0)
    qkv_bias = normal_values(key_list[6], (3 * D,), 0.3, 1.5, (), jnp.float32)
    proj_weight = normal_values(key_list[7], (D, D), D ** -0.5, 0.15625, ((0, 32),))
    proj_bias = normal_values(key_list[8], (D,), 0.3, 1.5, (), jnp.float32)
    merge_gain = jnp.clip(1.0 + 0.1 * jax.random.normal(key_list[9], (D,), jnp.float32), 0.5, 1.5)
    owner_keys = jax.random.split(jax.random.fold_in(key_list[10], 1), N_SECTION * (N_DEV * MERGED) // MERGED)
    owner_turns = jax.random.permutation(jax.random.fold_in(key_list[10], 3), N_SECTION * (N_DEV * MERGED) // MERGED)
    owner = jax.vmap(lambda own, number: shared_out(jax.random.fold_in(key_list[10], 2), own, number, MERGED, N_SECTION, 1, CAP, 2))(owner_keys, owner_turns).reshape((N_SECTION, N_DEV * MERGED, 1))
    return {"patches": patches, "win_count": win_count, "dest_perm": dest_perm, "win_groups": win_groups, "norm_gain": norm_gain, "qkv_weight": qkv_weight, "qkv_bias": qkv_bias, "proj_weight": proj_weight, "proj_bias": proj_bias, "merge_gain": merge_gain, "owner": owner}


def normalize(values, gain):
    return values * lax.rsqrt(lax.optimization_barrier(jnp.mean(values * values, axis=-1, keepdims=True)) + 1e-06) * gain

def encode(windows, groups, norm_gain, qkv_weight, qkv_bias, proj_weight, proj_bias, merge_gain):
    count = windows.shape[0]
    values = windows.reshape(count * WIN, D).astype(jnp.float32)
    normed = normalize(values, norm_gain).astype(jnp.bfloat16)
    triple = (jnp.dot(normed, qkv_weight, preferred_element_type=jnp.float32) + qkv_bias).astype(jnp.bfloat16)
    triple = triple.reshape(count, WIN, 3, HEADS, HEAD_DIM).astype(jnp.float32)
    scores = jnp.einsum('bqhe,bkhe->bhqk', triple[:, :, 0], triple[:, :, 1]) * HEAD_DIM ** (-0.5)
    living = jnp.arange(WIN, dtype=jnp.int32)[None, :] < 4 * groups[:, None]
    scores = jnp.where(living[:, None, None, :], scores, -1e+30)
    highest = lax.optimization_barrier(jnp.max(scores, axis=-1, keepdims=True))
    powers = jnp.exp(scores - highest)
    probs = (powers / lax.optimization_barrier(jnp.sum(powers, axis=-1, keepdims=True))).astype(jnp.bfloat16)
    mixed = jnp.einsum('bhqk,bkhe->bqhe', probs.astype(jnp.float32), triple[:, :, 2]).astype(jnp.bfloat16)
    mixed = mixed.reshape(count * WIN, D)
    encoded = values + jnp.dot(mixed, proj_weight, preferred_element_type=jnp.float32) + proj_bias
    final = normalize(encoded, merge_gain) * living.reshape(count * WIN, 1).astype(jnp.float32)
    return final.reshape(count * WIN // 4, 4 * D).astype(jnp.bfloat16)

def pack(merged, owners):
    sections = jnp.arange(N_SECTION, dtype=jnp.int32)
    hits = (owners[:, None] == sections[None, :]).astype(jnp.int32)
    ranks = lax.optimization_barrier(jnp.sum((jnp.cumsum(hits, axis=0) - hits) * hits, axis=1)).astype(jnp.int32)
    places = (owners * CAP + ranks).astype(jnp.int32)
    chosen = places[None, :] == jnp.arange(N_SECTION * CAP, dtype=jnp.int32)[:, None]
    ladder = jnp.arange(merged.shape[0], dtype=jnp.int32)
    indices = lax.optimization_barrier(jnp.sum(chosen.astype(jnp.int32) * ladder[None, :], axis=1)).astype(jnp.int32)
    filled = jnp.any(chosen, axis=1)
    return jnp.where(filled[:, None], merged[indices], jnp.zeros((), merged.dtype))

def reference(patches, win_count, dest_perm, win_groups, norm_gain, qkv_weight, qkv_bias, proj_weight, proj_bias, merge_gain, owner):
    buffers = []
    ladder = jnp.arange(N_DEV, dtype=jnp.int32)
    for section in range(N_SECTION):
        source_windows = patches[section].reshape(N_DEV, SRC_WIN, WIN, D)
        counts = win_count[section]
        before = lax.optimization_barrier(jnp.sum(jnp.where(ladder[None, :] < ladder[:, None], counts[None, :], 0), axis=1)).astype(jnp.int32)
        inverse = lax.optimization_barrier(jnp.sum(ladder[:, None] * (dest_perm[section][:, None] == ladder[None, :]).astype(jnp.int32), axis=0)).astype(jnp.int32)
        groups_table = win_groups[section]
        owner_table = owner[section, :, 0].reshape(N_DEV, MERGED)

        def one_device(target):
            wanted = (jnp.arange(DST_WIN, dtype=jnp.int32) * N_DEV + inverse[target]).astype(jnp.int32)
            source = (lax.optimization_barrier(jnp.sum((before[None, :] <= wanted[:, None]).astype(jnp.int32), axis=1)) - 1).astype(jnp.int32)
            within = (wanted - before[source]).astype(jnp.int32)
            merged = encode(source_windows[source, within], groups_table[source, within], norm_gain, qkv_weight, qkv_bias, proj_weight, proj_bias, merge_gain)
            return pack(merged, owner_table[target])
        buffers.append(lax.map(one_device, ladder))
    stacked = jnp.stack(buffers).reshape(N_SECTION, N_DEV, N_SECTION, CAP, 4 * D)
    return stacked.transpose(2, 1, 0, 3, 4).reshape(N_SECTION, N_DEV * N_SECTION * CAP, 4 * D)
```

```python
import functools

import jax
import jax.numpy as jnp
from jax import lax
from jax.experimental import pallas as pl
from jax.experimental.pallas import tpu as pltpu
from jax.sharding import Mesh
from jax.sharding import PartitionSpec as P

D = 1280
HEADS = 16
HD = 80
WIN = 64
DST_WIN = 8
SRC_WIN = 24
N_DEV = 32
N_SEC = 8
CAP = 32
ROWS = DST_WIN * WIN
MERGED = ROWS // 4
COLS = 4 * D
CHUNK = 640
HALF = 640
PAIR = 2 * WIN

F32 = jnp.float32
BF16 = jnp.bfloat16


def outgoing_kernel(place, counts, perm, patches, out, sem):
    pos = place[0]

    def add(d, total):
        return total + jnp.where(d < pos, counts[d], 0)

    begin = lax.fori_loop(0, N_DEV, add, jnp.int32(0))
    mine = counts[pos]

    def copy(i):
        slot = perm[jnp.bitwise_and(begin + i, N_DEV - 1)]
        return pltpu.make_async_copy(patches.at[i], out.at[slot], sem.at[i])

    for i in range(SRC_WIN):

        @pl.when(i < mine)
        def _(i=i):
            copy(i).start()

    for i in range(SRC_WIN):

        @pl.when(i < mine)
        def _(i=i):
            copy(i).wait()


def outgoing(place, counts, perm, patches):
    smem = pl.BlockSpec(memory_space=pltpu.SMEM)
    return pl.pallas_call(
        outgoing_kernel,
        out_shape=jax.ShapeDtypeStruct((N_DEV, WIN, D), patches.dtype),
        in_specs=[smem, smem, smem, pl.BlockSpec(memory_space=pl.ANY)],
        out_specs=pl.BlockSpec(memory_space=pl.ANY),
        scratch_shapes=[pltpu.SemaphoreType.DMA((SRC_WIN,))],
        name="outgoing",
    )(place, counts, perm, patches)


def lane_window(head):
    first = head * HD
    low = first // 128 * 128
    high = -(-(first + HD) // 128) * 128
    return first, low, high


def encode_kernel(
    n_pieces,
    place,
    counts,
    perm,
    groups,
    owner_row,
    owner_column,
    norm_gain,
    qkv_bias,
    proj_bias,
    merge_gain,
    arrived,
    *rest,
):
    pieces = rest[:n_pieces]
    out, weights, windows, normed, triple, mixed, encoded, source, live, wsem, xsem = rest[n_pieces:]
    pos = place[0]

    def weight_copy(n):
        row = pl.multiple_of(place[2 + 2 * n] * HALF, HALF)
        return pltpu.make_async_copy(
            pieces[n], weights.at[place[1 + 2 * n], pl.ds(row, HALF)], wsem.at[n]
        )

    def find(r, found):
        return jnp.where(perm[r] == pos, r, found)

    residue = lax.fori_loop(0, N_DEV, find, jnp.int32(0))

    def locate(d, begin):
        count = counts[d]
        within = jnp.bitwise_and(residue - begin, N_DEV - 1)

        @pl.when(within < count)
        def _():
            slot = lax.shift_right_logical(begin + within, 5)
            source[slot] = d
            live[slot] = 4 * groups[d * SRC_WIN + within]

        return begin + count

    lax.fori_loop(0, N_DEV, locate, jnp.int32(0))

    def window_copy(k):
        return pltpu.make_async_copy(
            arrived.at[source[k]], windows.at[pl.ds(k * WIN, WIN)], xsem.at[k]
        )

    for k in range(DST_WIN):
        window_copy(k).start()
    for n in range(n_pieces):
        weight_copy(n).start()
    for k in range(DST_WIN):
        window_copy(k).wait()
        rows = pl.ds(k * WIN, WIN)
        values = windows[rows, :].astype(F32)
        mean = jnp.mean(values * values, axis=-1, keepdims=True)
        normed[rows, :] = (values * lax.rsqrt(mean + 1e-6) * norm_gain[...]).astype(BF16)
    for n in range(n_pieces):
        weight_copy(n).wait()

    for c in range(6):
        cols = pl.ds(c * CHUNK, CHUNK)
        product = jnp.dot(normed[...], weights[c], preferred_element_type=F32)
        triple[c] = (product + qkv_bias[:, cols]).astype(BF16)

    query_at = lax.broadcasted_iota(jnp.int32, (PAIR, PAIR), 0)
    key_at = lax.broadcasted_iota(jnp.int32, (PAIR, PAIR), 1)

    def attend(pair, carry):
        rows = pl.ds(pl.multiple_of(pair * PAIR, PAIR), PAIR)
        first, second = live[2 * pair], live[2 * pair + 1]
        low = (query_at < WIN) & (key_at < first)
        high = (query_at >= WIN) & (key_at >= WIN) & (key_at < WIN + second)
        seen = low | high
        for half in range(2):
            parts = [jnp.zeros((PAIR, 128), F32) for _ in range(CHUNK // 128)]
            for head in range(HEADS // 2):
                begin, lo, hi = lane_window(head)
                lane = lo + lax.broadcasted_iota(jnp.int32, (PAIR, hi - lo), 1)
                inside = (lane >= begin) & (lane < begin + HD)
                zero = jnp.zeros((), BF16)
                q = jnp.where(inside, triple[half, rows, lo:hi], zero)
                k = triple[2 + half, rows, lo:hi]
                v = jnp.where(inside, triple[4 + half, rows, lo:hi], zero)
                scores = lax.dot_general(
                    q, k, (((1,), (1,)), ((), ())), preferred_element_type=F32
                )
                scores = jnp.where(seen, scores * HD ** (-0.5), -1e30)
                highest = jnp.max(scores, axis=-1, keepdims=True)
                powers = jnp.exp(scores - highest)
                probs = (powers / jnp.sum(powers, axis=-1, keepdims=True)).astype(BF16)
                product = jnp.dot(probs, v, preferred_element_type=F32)
                for tile in range(lo // 128, hi // 128):
                    at = tile * 128 - lo
                    parts[tile] = parts[tile] + product[:, at : at + 128]
            for tile in range(CHUNK // 128):
                at = half * CHUNK + tile * 128
                mixed[rows, at : at + 128] = parts[tile].astype(BF16)
        return carry

    lax.fori_loop(0, DST_WIN // 2, attend, 0)

    for half in range(2):
        cols = pl.ds(half * CHUNK, CHUNK)
        product = jnp.dot(mixed[...], weights[6 + half], preferred_element_type=F32)
        encoded[:, cols] = windows[:, cols].astype(F32) + product + proj_bias[:, cols]

    for k in range(DST_WIN):
        rows = pl.ds(k * WIN, WIN)
        values = encoded[rows, :]
        mean = jnp.mean(values * values, axis=-1, keepdims=True)
        alive = lax.broadcasted_iota(jnp.int32, (WIN, 1), 0) < live[k]
        scale = jnp.where(alive, lax.rsqrt(mean + 1e-6), 0.0)
        normed[rows, :] = (values * scale * merge_gain[...]).astype(BF16)

    lane = lax.broadcasted_iota(jnp.int32, (MERGED, ROWS), 1)
    earlier = lax.broadcasted_iota(jnp.int32, (MERGED, ROWS), 0) < lax.shift_right_logical(lane, 2)
    same = owner_column[...] == owner_row[...]
    rank = jnp.sum(jnp.where(same & earlier, 1, 0), axis=0, keepdims=True)
    places = owner_row[...] * CAP + rank
    chosen = lax.broadcasted_iota(jnp.int32, (N_SEC * CAP, ROWS), 0) == places
    turn = jnp.bitwise_and(lax.broadcasted_iota(jnp.int32, (N_SEC * CAP, ROWS), 1), 3)
    for p in range(4):
        pick = jnp.where(chosen & (turn == p), 1.0, 0.0).astype(BF16)
        packed = jnp.dot(pick, normed[...], preferred_element_type=F32)
        out[:, p * D : (p + 1) * D] = packed.astype(BF16)


def encode(place, counts, perm, groups, owner_row, owner_column, gain, qb, pb, mg, arrived, pieces):
    smem = pl.BlockSpec(memory_space=pltpu.SMEM)
    vmem = pl.BlockSpec(memory_space=pltpu.VMEM)
    hbm = pl.BlockSpec(memory_space=pl.ANY)
    n = len(pieces)
    return pl.pallas_call(
        functools.partial(encode_kernel, n),
        out_shape=jax.ShapeDtypeStruct((N_SEC * CAP, COLS), BF16),
        in_specs=[smem] * 4 + [vmem] * 6 + [hbm] * (1 + n),
        out_specs=vmem,
        scratch_shapes=[
            pltpu.VMEM((8, D, CHUNK), BF16),
            pltpu.VMEM((ROWS, D), BF16),
            pltpu.VMEM((ROWS, D), BF16),
            pltpu.VMEM((6, ROWS, CHUNK), BF16),
            pltpu.VMEM((ROWS, D), BF16),
            pltpu.VMEM((ROWS, D), F32),
            pltpu.SMEM((DST_WIN,), jnp.int32),
            pltpu.SMEM((DST_WIN,), jnp.int32),
            pltpu.SemaphoreType.DMA((n,)),
            pltpu.SemaphoreType.DMA((DST_WIN,)),
        ],
        compiler_params=pltpu.CompilerParams(vmem_limit_bytes=48 * 1024 * 1024),
        name="encode",
    )(place, counts, perm, groups, owner_row, owner_column, gain, qb, pb, mg, arrived, *pieces)


def shift(n, k):
    return [(i, (i + k) % n) for i in range(n)]


SWAP = [(0, 1), (1, 0)]
CROSS = [(i, 3 - i) for i in range(4)]


def gather_weights(qkv_weight, proj_weight):
    y, xh = lax.axis_index("y"), lax.axis_index("xh")
    c = lax.axis_index("c")
    send = lax.ppermute
    shard = jnp.concatenate([qkv_weight, proj_weight], axis=1)
    other = send(shard, "c", SWAP)
    slab = jnp.concatenate([jnp.where(c == 0, shard, other), jnp.where(c == 0, other, shard)], axis=0)
    own = lax.dynamic_slice(slab, (0, (2 * y + c) * CHUNK), (80, CHUNK))
    here = lax.all_to_all(jnp.broadcast_to(own[None], (8, 80, CHUNK)), "z", 0, 0, tiled=True)
    here = here.reshape(HALF, CHUNK)
    across = send(here, ("xl", "xh"), CROSS)
    up_h, down_h = send(here, "y", shift(4, 1)), send(here, "y", shift(4, -1))
    up_a, down_a = send(across, "y", shift(4, 1)), send(across, "y", shift(4, -1))
    far_h, far_a = send(up_h, "y", shift(4, 1)), send(down_a, "y", shift(4, -1))
    pieces = [here, across, up_h, down_h, up_a, down_a, far_h, far_a]
    steps = [0, 0, 1, -1, 1, -1, 2, 2]
    halves = [xh, 1 - xh, xh, xh, 1 - xh, 1 - xh, xh, 1 - xh]
    placed = []
    for core in (c, 1 - c):
        for step, half in zip(steps, halves):
            placed += [jnp.mod(y - step, 4) * 2 + core, half]
    return pieces + [send(p, "c", SWAP) for p in pieces], placed


def body(
    patches,
    win_count,
    dest_perm,
    win_groups,
    norm_gain,
    qkv_weight,
    qkv_bias,
    proj_weight,
    proj_bias,
    merge_gain,
    owner,
):
    position = lax.axis_index(("xh", "z", "c"))
    counts, perm = win_count[0], dest_perm[0]
    pieces, placed = gather_weights(qkv_weight, proj_weight)
    place = jnp.stack([position] + placed).astype(jnp.int32)
    going = outgoing(
        position.astype(jnp.int32).reshape(1), counts, perm, patches.reshape(SRC_WIN, WIN, D)
    )
    arrived = lax.all_to_all(going, ("xh", "z", "c"), split_axis=0, concat_axis=0, tiled=True)
    packed = encode(
        place,
        counts,
        perm,
        win_groups.reshape(N_DEV * SRC_WIN),
        jnp.repeat(owner.reshape(1, MERGED), 4, axis=1),
        owner.reshape(MERGED, 1),
        norm_gain.reshape(1, D),
        qkv_bias.reshape(1, 3 * D),
        proj_bias.reshape(1, D),
        merge_gain.reshape(1, D),
        arrived,
        pieces,
    )
    delivered = lax.all_to_all(packed, ("y", "xl"), split_axis=0, concat_axis=0, tiled=True)
    return delivered.reshape(1, N_SEC * CAP, COLS)


def solution(mesh):
    fine = Mesh(mesh.devices.reshape(4, 2, 2, 8, 2), ("y", "xl", "xh", "z", "c"))
    sec, dev = ("y", "xl"), ("xh", "z", "c")
    return jax.shard_map(
        body,
        mesh=fine,
        in_specs=(
            P(sec, dev, None),
            P(sec, None),
            P(sec, None),
            P(sec, None, None),
            P(),
            P(dev, None),
            P(),
            P(dev, None),
            P(),
            P(),
            P(sec, dev, None),
        ),
        out_specs=P(sec, dev, None),
        check_vma=False,
    )
```

```python
import functools

import jax
import jax.numpy as jnp
from jax import lax
from jax.experimental import pallas as pl
from jax.experimental.pallas import tpu as pltpu
from jax.sharding import Mesh
from jax.sharding import PartitionSpec as P

D = 1280
HEADS = 16
HD = 80
WIN = 64
DST_WIN = 8
SRC_WIN = 24
N_DEV = 32
N_SEC = 8
CAP = 32
ROWS = DST_WIN * WIN
MERGED = ROWS // 4
COLS = 4 * D
CHUNK = 640
HALF = 640
PAIR = 2 * WIN

F32 = jnp.float32
BF16 = jnp.bfloat16


def outgoing_kernel(place, counts, perm, patches, out, staged, in_sem, out_sem):
    pos = place[0]
    mine = counts[pos]

    def load(i):
        return pltpu.make_async_copy(patches.at[i], staged.at[i], in_sem.at[i])

    for i in range(SRC_WIN):

        @pl.when(i < mine)
        def _(i=i):
            load(i).start()

    def add(d, total):
        return total + jnp.where(d < pos, counts[d], 0)

    begin = lax.fori_loop(0, N_DEV, add, jnp.int32(0))

    def save(i):
        slot = perm[jnp.bitwise_and(begin + i, N_DEV - 1)]
        return pltpu.make_async_copy(staged.at[i], out.at[slot], out_sem.at[i])

    for i in range(SRC_WIN):

        @pl.when(i < mine)
        def _(i=i):
            load(i).wait()
            save(i).start()

    for i in range(SRC_WIN):

        @pl.when(i < mine)
        def _(i=i):
            save(i).wait()


def outgoing(place, counts, perm, patches):
    smem = pl.BlockSpec(memory_space=pltpu.SMEM)
    return pl.pallas_call(
        outgoing_kernel,
        out_shape=jax.ShapeDtypeStruct((N_DEV, WIN, D), patches.dtype),
        in_specs=[smem, smem, smem, pl.BlockSpec(memory_space=pl.ANY)],
        out_specs=pl.BlockSpec(memory_space=pl.ANY),
        scratch_shapes=[
            pltpu.VMEM((SRC_WIN, WIN, D), patches.dtype),
            pltpu.SemaphoreType.DMA((SRC_WIN,)),
            pltpu.SemaphoreType.DMA((SRC_WIN,)),
        ],
        compiler_params=pltpu.CompilerParams(vmem_limit_bytes=16 * 1024 * 1024),
        name="outgoing",
    )(place, counts, perm, patches)


def lane_window(head):
    first = head * HD
    low = first // 128 * 128
    high = -(-(first + HD) // 128) * 128
    return first, low, high


def encode_kernel(
    n_pieces,
    place,
    counts,
    perm,
    groups,
    owner_row,
    owner_column,
    norm_gain,
    qkv_bias,
    proj_bias,
    merge_gain,
    arrived,
    *rest,
):
    pieces = rest[:n_pieces]
    out, weights, windows, normed, triple, mixed, encoded, source, live, wsem, xsem = rest[n_pieces:]
    pos = place[0]

    def weight_copy(n):
        row = pl.multiple_of(place[2 + 2 * n] * HALF, HALF)
        return pltpu.make_async_copy(
            pieces[n], weights.at[place[1 + 2 * n], pl.ds(row, HALF)], wsem.at[n]
        )

    def find(r, found):
        return jnp.where(perm[r] == pos, r, found)

    residue = lax.fori_loop(0, N_DEV, find, jnp.int32(0))

    def locate(d, begin):
        count = counts[d]
        within = jnp.bitwise_and(residue - begin, N_DEV - 1)

        @pl.when(within < count)
        def _():
            slot = lax.shift_right_logical(begin + within, 5)
            source[slot] = d
            live[slot] = 4 * groups[d * SRC_WIN + within]

        return begin + count

    lax.fori_loop(0, N_DEV, locate, jnp.int32(0))

    def window_copy(k):
        return pltpu.make_async_copy(
            arrived.at[source[k]], windows.at[pl.ds(k * WIN, WIN)], xsem.at[k]
        )

    for k in range(DST_WIN):
        window_copy(k).start()
    for n in range(n_pieces):
        weight_copy(n).start()
    for k in range(DST_WIN):
        window_copy(k).wait()
        rows = pl.ds(k * WIN, WIN)
        values = windows[rows, :].astype(F32)
        mean = jnp.mean(values * values, axis=-1, keepdims=True)
        normed[rows, :] = (values * lax.rsqrt(mean + 1e-6) * norm_gain[...]).astype(BF16)
    for n in range(n_pieces):
        weight_copy(n).wait()

    for c in range(6):
        cols = pl.ds(c * CHUNK, CHUNK)
        product = jnp.dot(normed[...], weights[c], preferred_element_type=F32)
        triple[c] = (product + qkv_bias[:, cols]).astype(BF16)

    query_at = lax.broadcasted_iota(jnp.int32, (PAIR, PAIR), 0)
    key_at = lax.broadcasted_iota(jnp.int32, (PAIR, PAIR), 1)

    def attend(pair, carry):
        rows = pl.ds(pl.multiple_of(pair * PAIR, PAIR), PAIR)
        first, second = live[2 * pair], live[2 * pair + 1]
        low = (query_at < WIN) & (key_at < first)
        high = (query_at >= WIN) & (key_at >= WIN) & (key_at < WIN + second)
        seen = low | high
        for half in range(2):
            parts = [jnp.zeros((PAIR, 128), F32) for _ in range(CHUNK // 128)]
            for head in range(HEADS // 2):
                begin, lo, hi = lane_window(head)
                lane = lo + lax.broadcasted_iota(jnp.int32, (PAIR, hi - lo), 1)
                inside = (lane >= begin) & (lane < begin + HD)
                zero = jnp.zeros((), BF16)
                q = jnp.where(inside, triple[half, rows, lo:hi], zero)
                k = triple[2 + half, rows, lo:hi]
                v = jnp.where(inside, triple[4 + half, rows, lo:hi], zero)
                scores = lax.dot_general(
                    q, k, (((1,), (1,)), ((), ())), preferred_element_type=F32
                )
                scores = jnp.where(seen, scores * HD ** (-0.5), -1e30)
                highest = jnp.max(scores, axis=-1, keepdims=True)
                powers = jnp.exp(scores - highest)
                probs = (powers / jnp.sum(powers, axis=-1, keepdims=True)).astype(BF16)
                product = jnp.dot(probs, v, preferred_element_type=F32)
                for tile in range(lo // 128, hi // 128):
                    at = tile * 128 - lo
                    parts[tile] = parts[tile] + product[:, at : at + 128]
            for tile in range(CHUNK // 128):
                at = half * CHUNK + tile * 128
                mixed[rows, at : at + 128] = parts[tile].astype(BF16)
        return carry

    lax.fori_loop(0, DST_WIN // 2, attend, 0)

    for half in range(2):
        cols = pl.ds(half * CHUNK, CHUNK)
        product = jnp.dot(mixed[...], weights[6 + half], preferred_element_type=F32)
        encoded[:, cols] = windows[:, cols].astype(F32) + product + proj_bias[:, cols]

    for k in range(DST_WIN):
        rows = pl.ds(k * WIN, WIN)
        values = encoded[rows, :]
        mean = jnp.mean(values * values, axis=-1, keepdims=True)
        alive = lax.broadcasted_iota(jnp.int32, (WIN, 1), 0) < live[k]
        scale = jnp.where(alive, lax.rsqrt(mean + 1e-6), 0.0)
        normed[rows, :] = (values * scale * merge_gain[...]).astype(BF16)

    lane = lax.broadcasted_iota(jnp.int32, (MERGED, ROWS), 1)
    earlier = lax.broadcasted_iota(jnp.int32, (MERGED, ROWS), 0) < lax.shift_right_logical(lane, 2)
    same = owner_column[...] == owner_row[...]
    rank = jnp.sum(jnp.where(same & earlier, 1, 0), axis=0, keepdims=True)
    places = owner_row[...] * CAP + rank
    chosen = lax.broadcasted_iota(jnp.int32, (N_SEC * CAP, ROWS), 0) == places
    turn = jnp.bitwise_and(lax.broadcasted_iota(jnp.int32, (N_SEC * CAP, ROWS), 1), 3)
    for p in range(4):
        pick = jnp.where(chosen & (turn == p), 1.0, 0.0).astype(BF16)
        packed = jnp.dot(pick, normed[...], preferred_element_type=F32)
        out[:, p * D : (p + 1) * D] = packed.astype(BF16)


def encode(place, counts, perm, groups, owner_row, owner_column, gain, qb, pb, mg, arrived, pieces):
    smem = pl.BlockSpec(memory_space=pltpu.SMEM)
    vmem = pl.BlockSpec(memory_space=pltpu.VMEM)
    hbm = pl.BlockSpec(memory_space=pl.ANY)
    n = len(pieces)
    return pl.pallas_call(
        functools.partial(encode_kernel, n),
        out_shape=jax.ShapeDtypeStruct((N_SEC * CAP, COLS), BF16),
        in_specs=[smem] * 4 + [vmem] * 6 + [hbm] * (1 + n),
        out_specs=vmem,
        scratch_shapes=[
            pltpu.VMEM((8, D, CHUNK), BF16),
            pltpu.VMEM((ROWS, D), BF16),
            pltpu.VMEM((ROWS, D), BF16),
            pltpu.VMEM((6, ROWS, CHUNK), BF16),
            pltpu.VMEM((ROWS, D), BF16),
            pltpu.VMEM((ROWS, D), F32),
            pltpu.SMEM((DST_WIN,), jnp.int32),
            pltpu.SMEM((DST_WIN,), jnp.int32),
            pltpu.SemaphoreType.DMA((n,)),
            pltpu.SemaphoreType.DMA((DST_WIN,)),
        ],
        compiler_params=pltpu.CompilerParams(vmem_limit_bytes=48 * 1024 * 1024),
        name="encode",
    )(place, counts, perm, groups, owner_row, owner_column, gain, qb, pb, mg, arrived, *pieces)


def shift(n, k):
    return [(i, (i + k) % n) for i in range(n)]


SWAP = [(0, 1), (1, 0)]
CROSS = [(i, 3 - i) for i in range(4)]


def gather_weights(qkv_weight, proj_weight):
    y, xh = lax.axis_index("y"), lax.axis_index("xh")
    c = lax.axis_index("c")
    send = lax.ppermute
    shard = jnp.concatenate([qkv_weight, proj_weight], axis=1)
    other = send(shard, "c", SWAP)
    slab = jnp.concatenate([jnp.where(c == 0, shard, other), jnp.where(c == 0, other, shard)], axis=0)
    own = lax.dynamic_slice(slab, (0, (2 * y + c) * CHUNK), (80, CHUNK))
    here = lax.all_to_all(jnp.broadcast_to(own[None], (8, 80, CHUNK)), "z", 0, 0, tiled=True)
    here = here.reshape(HALF, CHUNK)
    across = send(here, ("xl", "xh"), CROSS)
    up_h, down_h = send(here, "y", shift(4, 1)), send(here, "y", shift(4, -1))
    up_a, down_a = send(across, "y", shift(4, 1)), send(across, "y", shift(4, -1))
    far_h, far_a = send(up_h, "y", shift(4, 1)), send(down_a, "y", shift(4, -1))
    pieces = [here, across, up_h, down_h, up_a, down_a, far_h, far_a]
    steps = [0, 0, 1, -1, 1, -1, 2, 2]
    halves = [xh, 1 - xh, xh, xh, 1 - xh, 1 - xh, xh, 1 - xh]
    placed = []
    for core in (c, 1 - c):
        for step, half in zip(steps, halves):
            placed += [jnp.mod(y - step, 4) * 2 + core, half]
    return pieces + [send(p, "c", SWAP) for p in pieces], placed


def body(
    patches,
    win_count,
    dest_perm,
    win_groups,
    norm_gain,
    qkv_weight,
    qkv_bias,
    proj_weight,
    proj_bias,
    merge_gain,
    owner,
):
    position = lax.axis_index(("xh", "z", "c"))
    counts, perm = win_count[0], dest_perm[0]
    pieces, placed = gather_weights(qkv_weight, proj_weight)
    place = jnp.stack([position] + placed).astype(jnp.int32)
    going = outgoing(
        position.astype(jnp.int32).reshape(1), counts, perm, patches.reshape(SRC_WIN, WIN, D)
    )
    arrived = lax.all_to_all(going, ("xh", "z", "c"), split_axis=0, concat_axis=0, tiled=True)
    packed = encode(
        place,
        counts,
        perm,
        win_groups.reshape(N_DEV * SRC_WIN),
        jnp.repeat(owner.reshape(1, MERGED), 4, axis=1),
        owner.reshape(MERGED, 1),
        norm_gain.reshape(1, D),
        qkv_bias.reshape(1, 3 * D),
        proj_bias.reshape(1, D),
        merge_gain.reshape(1, D),
        arrived,
        pieces,
    )
    delivered = lax.all_to_all(packed, ("y", "xl"), split_axis=0, concat_axis=0, tiled=True)
    return delivered.reshape(1, N_SEC * CAP, COLS)


def solution(mesh):
    fine = Mesh(mesh.devices.reshape(4, 2, 2, 8, 2), ("y", "xl", "xh", "z", "c"))
    sec, dev = ("y", "xl"), ("xh", "z", "c")
    return jax.shard_map(
        body,
        mesh=fine,
        in_specs=(
            P(sec, dev, None),
            P(sec, None),
            P(sec, None),
            P(sec, None, None),
            P(),
            P(dev, None),
            P(),
            P(dev, None),
            P(),
            P(),
            P(sec, dev, None),
        ),
        out_specs=P(sec, dev, None),
        check_vma=False,
    )
```

```python
import math

import jax
import jax.numpy as jnp
from jax import lax
from jax.experimental import pallas as pl
from jax.experimental.pallas import tpu as pltpu
from jax.sharding import Mesh
from jax.sharding import PartitionSpec as P

D = 1280
HEADS = 16
HD = 80
WIN = 64
DST_WIN = 8
SRC_WIN = 24
N_DEV = 32
N_SEC = 8
CAP = 32
ROWS = DST_WIN * WIN
MERGED = ROWS // 4
COLS = 4 * D
CHUNK = 640
HALF = 640
EXP2_SCALE = HD ** (-0.5) * math.log2(math.e)
VMEM_LIMIT = 48 * 1024 * 1024

F32 = jnp.float32
BF16 = jnp.bfloat16


def outgoing_kernel(place, counts, perm, patches, out, staged, in_sem, out_sem):
    pos = place[0]
    mine = counts[pos]

    def load(i):
        return pltpu.make_async_copy(patches.at[i], staged.at[i], in_sem.at[i])

    for i in range(SRC_WIN):

        @pl.when(i < mine)
        def _(i=i):
            load(i).start()

    def add(d, total):
        return total + jnp.where(d < pos, counts[d], 0)

    begin = lax.fori_loop(0, N_DEV, add, jnp.int32(0))

    def save(i):
        slot = perm[jnp.bitwise_and(begin + i, N_DEV - 1)]
        return pltpu.make_async_copy(staged.at[i], out.at[slot], out_sem.at[i])

    for i in range(SRC_WIN):

        @pl.when(i < mine)
        def _(i=i):
            load(i).wait()
            save(i).start()

    for i in range(SRC_WIN):

        @pl.when(i < mine)
        def _(i=i):
            save(i).wait()


def outgoing(place, counts, perm, patches):
    smem = pl.BlockSpec(memory_space=pltpu.SMEM)
    return pl.pallas_call(
        outgoing_kernel,
        out_shape=jax.ShapeDtypeStruct((N_DEV, WIN, D), patches.dtype),
        in_specs=[smem, smem, smem, pl.BlockSpec(memory_space=pl.ANY)],
        out_specs=pl.BlockSpec(memory_space=pl.ANY),
        scratch_shapes=[
            pltpu.VMEM((SRC_WIN, WIN, D), patches.dtype),
            pltpu.SemaphoreType.DMA((SRC_WIN,)),
            pltpu.SemaphoreType.DMA((SRC_WIN,)),
        ],
        compiler_params=pltpu.CompilerParams(vmem_limit_bytes=16 * 1024 * 1024),
        name="outgoing",
    )(place, counts, perm, patches)


def encode_kernel(
    place,
    counts,
    perm,
    groups,
    owner_row,
    owner_column,
    norm_gain,
    qkv_bias,
    proj_bias,
    merge_gain,
    arrived,
    *rest,
):
    pieces = rest[:16]
    out, weights, windows, normed, triple, mixed, encoded, final, source, live, wsem, xsem = rest[16:]
    pos, here, side = place[0], place[1], place[2]

    def find(r, found):
        return jnp.where(perm[r] == pos, r, found)

    residue = lax.fori_loop(0, N_DEV, find, jnp.int32(0))

    def locate(d, begin):
        count = counts[d]
        within = jnp.bitwise_and(residue - begin, N_DEV - 1)

        @pl.when(within < count)
        def _():
            slot = lax.shift_right_logical(begin + within, 5)
            source[slot] = d
            live[slot] = 4 * groups[d * SRC_WIN + within]

        return begin + count

    lax.fori_loop(0, N_DEV, locate, jnp.int32(0))

    def window_copy(k):
        return pltpu.make_async_copy(
            arrived.at[source[k]], windows.at[pl.ds(k * WIN, WIN)], xsem.at[k]
        )

    def weight_copy(n, core, across):
        row = jnp.bitwise_xor(here, across) * HALF
        column = jnp.bitwise_xor(side, core) * CHUNK
        to = weights.at[
            place[3 + n],
            pl.ds(pl.multiple_of(row, HALF), HALF),
            pl.ds(pl.multiple_of(column, CHUNK), CHUNK),
        ]
        return pltpu.make_async_copy(pieces[8 * core + 2 * n + across], to, wsem.at[n, core, across])

    for k in range(DST_WIN):
        window_copy(k).start()
    for n in range(4):
        for core in range(2):
            for across in range(2):
                weight_copy(n, core, across).start()
    for k in range(DST_WIN):
        window_copy(k).wait()
        rows = pl.ds(k * WIN, WIN)
        values = windows[rows, :].astype(F32)
        mean = jnp.mean(values * values, axis=-1, keepdims=True)
        normed[rows, :] = (values * lax.rsqrt(mean + 1e-6) * norm_gain[...]).astype(BF16)

    for n in range(4):
        block = place[3 + n]
        for core in range(2):
            for across in range(2):
                weight_copy(n, core, across).wait()

        @pl.when(block < 3)
        def _(block=block):
            product = jnp.dot(normed[...], weights[block], preferred_element_type=F32)
            triple[block] = (product + qkv_bias[block]).astype(BF16)

    def attend(w, carry):
        rows = pl.ds(pl.multiple_of(w * WIN, WIN), WIN)
        dead = lax.broadcasted_iota(jnp.int32, (WIN, 2 * WIN), 0) >= live[w]
        zero = jnp.zeros((), BF16)
        for half in range(2):
            parts = [None] * (CHUNK // 128)
            for pair in range(HEADS // 4):
                begin = pair * 2 * HD
                low = begin // 128 * 128
                lane = low + lax.broadcasted_iota(jnp.int32, (WIN, 256), 1)
                first = (lane >= begin) & (lane < begin + HD)
                second = (lane >= begin + HD) & (lane < begin + 2 * HD)
                at = half * CHUNK + low
                q = triple[0, rows, at : at + 256]
                k = triple[1, rows, at : at + 256]
                v = triple[2, rows, at : at + 256]
                both = jnp.concatenate([jnp.where(first, q, zero), jnp.where(second, q, zero)], axis=0)
                scores = lax.dot_general(
                    k, both, (((1,), (1,)), ((), ())), preferred_element_type=F32
                )
                scores = jnp.where(dead, -1e30, scores)
                highest = jnp.max(scores, axis=0, keepdims=True)
                powers = jnp.exp2((scores - highest) * EXP2_SCALE)
                probs = powers * (1.0 / jnp.sum(powers, axis=0, keepdims=True))
                product = lax.dot_general(
                    probs.astype(BF16), v, (((0,), (0,)), ((), ())), preferred_element_type=F32
                )
                product = jnp.where(first, product[:WIN], jnp.where(second, product[WIN:], 0.0))
                for t in range(2):
                    tile, part = low // 128 + t, product[:, 128 * t : 128 * t + 128]
                    parts[tile] = part if parts[tile] is None else parts[tile] + part
            for tile in range(CHUNK // 128):
                at = half * CHUNK + tile * 128
                mixed[rows, at : at + 128] = parts[tile].astype(BF16)
        return carry

    lax.fori_loop(0, DST_WIN, attend, 0)

    encoded[...] = jnp.dot(mixed[...], weights[3], preferred_element_type=F32)
    for k in range(DST_WIN):
        rows = pl.ds(k * WIN, WIN)
        values = windows[rows, :].astype(F32) + encoded[rows, :] + proj_bias[...]
        mean = jnp.mean(values * values, axis=-1, keepdims=True)
        alive = lax.broadcasted_iota(jnp.int32, (WIN, 1), 0) < live[k]
        scale = jnp.where(alive, lax.rsqrt(mean + 1e-6), 0.0)
        final[rows, :] = (values * scale * merge_gain[...]).astype(BF16)

    lane = lax.broadcasted_iota(jnp.int32, (MERGED, ROWS), 1)
    earlier = lax.broadcasted_iota(jnp.int32, (MERGED, ROWS), 0) < lax.shift_right_logical(lane, 2)
    same = owner_column[...] == owner_row[...]
    rank = jnp.sum(jnp.where(same & earlier, 1, 0), axis=0, keepdims=True)
    places = owner_row[...] * CAP + rank
    chosen = lax.broadcasted_iota(jnp.int32, (N_SEC * CAP, ROWS), 0) == places
    turn = jnp.bitwise_and(lax.broadcasted_iota(jnp.int32, (N_SEC * CAP, ROWS), 1), 3)
    for p in range(4):
        pick = jnp.where(chosen & (turn == p), 1.0, 0.0).astype(BF16)
        packed = jnp.dot(pick, final[...], preferred_element_type=F32)
        out[:, p * D : (p + 1) * D] = packed.astype(BF16)


def encode(place, counts, perm, groups, owner_row, owner_column, gain, qb, pb, mg, arrived, pieces):
    smem = pl.BlockSpec(memory_space=pltpu.SMEM)
    vmem = pl.BlockSpec(memory_space=pltpu.VMEM)
    hbm = pl.BlockSpec(memory_space=pl.ANY)
    return pl.pallas_call(
        encode_kernel,
        out_shape=jax.ShapeDtypeStruct((N_SEC * CAP, COLS), BF16),
        in_specs=[smem] * 4 + [vmem] * 6 + [hbm] * 17,
        out_specs=vmem,
        scratch_shapes=[
            pltpu.VMEM((4, D, D), BF16),
            pltpu.VMEM((ROWS, D), BF16),
            pltpu.VMEM((ROWS, D), BF16),
            pltpu.VMEM((3, ROWS, D), BF16),
            pltpu.VMEM((ROWS, D), BF16),
            pltpu.VMEM((ROWS, D), F32),
            pltpu.VMEM((ROWS, D), BF16),
            pltpu.SMEM((DST_WIN,), jnp.int32),
            pltpu.SMEM((DST_WIN,), jnp.int32),
            pltpu.SemaphoreType.DMA((4, 2, 2)),
            pltpu.SemaphoreType.DMA((DST_WIN,)),
        ],
        compiler_params=pltpu.CompilerParams(vmem_limit_bytes=VMEM_LIMIT),
        name="encode",
    )(place, counts, perm, groups, owner_row, owner_column, gain, qb, pb, mg, arrived, *pieces)


def shift(n, k):
    return [(i, (i + k) % n) for i in range(n)]


SWAP = [(0, 1), (1, 0)]
CROSS = [(i, 3 - i) for i in range(4)]
CROSS3 = [(i, 7 - i) for i in range(8)]


def gather_weights(qkv_weight, proj_weight):
    y, xl, c = lax.axis_index("y"), lax.axis_index("xl"), lax.axis_index("c")
    send = lax.ppermute
    side = jnp.bitwise_xor(xl, c)
    chunk = 2 * y + side
    from_qkv = lax.dynamic_slice(qkv_weight, (0, jnp.minimum(chunk, 5) * CHUNK), (40, CHUNK))
    from_proj = lax.dynamic_slice(proj_weight, (0, jnp.maximum(chunk - 6, 0) * CHUNK), (40, CHUNK))
    own = jnp.where(chunk < 6, from_qkv, from_proj)
    column = lax.all_to_all(jnp.broadcast_to(own[None], (8, 40, CHUNK)), "z", 0, 0, tiled=True)
    return column, side


def spread_weights(column, side):
    y, xh, c = lax.axis_index("y"), lax.axis_index("xh"), lax.axis_index("c")
    send = lax.ppermute
    partner = send(column, ("xl", "c"), CROSS)
    low, high = jnp.where(c == 0, column, partner), jnp.where(c == 0, partner, column)
    here = jnp.concatenate([low, high], axis=1).reshape(HALF, CHUNK)
    across = send(here, ("xl", "xh", "c"), CROSS3)
    up_h, down_h = send(here, "y", shift(4, 1)), send(here, "y", shift(4, -1))
    up_a, down_a = send(across, "y", shift(4, 1)), send(across, "y", shift(4, -1))
    far_h, far_a = send(up_h, "y", shift(4, 1)), send(down_a, "y", shift(4, -1))
    pieces = [here, across, up_h, up_a, down_h, down_a, far_h, far_a]
    pieces = pieces + [send(p, "c", SWAP) for p in pieces]
    return pieces, [xh, side] + [jnp.mod(y - step, 4) for step in (0, 1, -1, 2)]


def body(
    patches,
    win_count,
    dest_perm,
    win_groups,
    norm_gain,
    qkv_weight,
    qkv_bias,
    proj_weight,
    proj_bias,
    merge_gain,
    owner,
):
    position = lax.axis_index(("xh", "z", "c"))
    counts, perm = win_count[0], dest_perm[0]
    column, side = gather_weights(qkv_weight, proj_weight)
    going = outgoing(
        position.astype(jnp.int32).reshape(1), counts, perm, patches.reshape(SRC_WIN, WIN, D)
    )
    pieces, placed = spread_weights(column, side)
    place = jnp.stack([position] + placed).astype(jnp.int32)
    arrived = lax.all_to_all(going, ("xh", "z", "c"), split_axis=0, concat_axis=0, tiled=True)
    packed = encode(
        place,
        counts,
        perm,
        win_groups.reshape(N_DEV * SRC_WIN),
        jnp.repeat(owner.reshape(1, MERGED), 4, axis=1),
        owner.reshape(MERGED, 1),
        norm_gain.reshape(1, D),
        qkv_bias.reshape(3, 1, D),
        proj_bias.reshape(1, D),
        merge_gain.reshape(1, D),
        arrived,
        pieces,
    )
    delivered = lax.all_to_all(packed, ("y", "xl"), split_axis=0, concat_axis=0, tiled=True)
    return delivered.reshape(1, N_SEC * CAP, COLS)


def solution(mesh):
    fine = Mesh(mesh.devices.reshape(4, 2, 2, 8, 2), ("y", "xl", "xh", "z", "c"))
    sec, dev = ("y", "xl"), ("xh", "z", "c")
    return jax.shard_map(
        body,
        mesh=fine,
        in_specs=(
            P(sec, dev, None),
            P(sec, None),
            P(sec, None),
            P(sec, None, None),
            P(),
            P(dev, None),
            P(),
            P(dev, None),
            P(),
            P(),
            P(sec, dev, None),
        ),
        out_specs=P(sec, dev, None),
        check_vma=False,
    )
```

```python
import math

import jax
import jax.numpy as jnp
from jax import lax
from jax.experimental import pallas as pl
from jax.experimental.pallas import tpu as pltpu
from jax.sharding import Mesh
from jax.sharding import PartitionSpec as P

D = 1280
HEADS = 16
HD = 80
WIN = 64
DST_WIN = 8
SRC_WIN = 24
N_DEV = 32
N_SEC = 8
CAP = 32
ROWS = DST_WIN * WIN
MERGED = ROWS // 4
COLS = 4 * D
CHUNK = 640
HALF = 640
EXP2_SCALE = HD ** (-0.5) * math.log2(math.e)
VMEM_LIMIT = 48 * 1024 * 1024

F32 = jnp.float32
BF16 = jnp.bfloat16


def outgoing_kernel(place, counts, perm, patches, out, staged, in_sem, out_sem):
    pos = place[0]
    mine = counts[pos]

    def load(i):
        return pltpu.make_async_copy(patches.at[i], staged.at[i], in_sem.at[i])

    for i in range(SRC_WIN):

        @pl.when(i < mine)
        def _(i=i):
            load(i).start()

    def add(d, total):
        return total + jnp.where(d < pos, counts[d], 0)

    begin = lax.fori_loop(0, N_DEV, add, jnp.int32(0))

    def save(i):
        slot = perm[jnp.bitwise_and(begin + i, N_DEV - 1)]
        return pltpu.make_async_copy(staged.at[i], out.at[slot], out_sem.at[i])

    for i in range(SRC_WIN):

        @pl.when(i < mine)
        def _(i=i):
            load(i).wait()
            save(i).start()

    for i in range(SRC_WIN):

        @pl.when(i < mine)
        def _(i=i):
            save(i).wait()


def outgoing(place, counts, perm, patches):
    smem = pl.BlockSpec(memory_space=pltpu.SMEM)
    return pl.pallas_call(
        outgoing_kernel,
        out_shape=jax.ShapeDtypeStruct((N_DEV, WIN, D), patches.dtype),
        in_specs=[smem, smem, smem, pl.BlockSpec(memory_space=pltpu.HBM)],
        out_specs=pl.BlockSpec(memory_space=pltpu.HBM),
        scratch_shapes=[
            pltpu.VMEM((SRC_WIN, WIN, D), patches.dtype),
            pltpu.SemaphoreType.DMA((SRC_WIN,)),
            pltpu.SemaphoreType.DMA((SRC_WIN,)),
        ],
        compiler_params=pltpu.CompilerParams(vmem_limit_bytes=60 * 1024 * 1024),
        name="outgoing",
    )(place, counts, perm, patches)


def encode_kernel(
    place,
    counts,
    perm,
    groups,
    owner_row,
    owner_column,
    norm_gain,
    qkv_bias,
    proj_bias,
    merge_gain,
    arrived,
    *rest,
):
    pieces = rest[:16]
    out, weights, windows, normed, triple, mixed, encoded, final, source, live, wsem, xsem = rest[16:]
    pos, here, side = place[0], place[1], place[2]

    def find(r, found):
        return jnp.where(perm[r] == pos, r, found)

    residue = lax.fori_loop(0, N_DEV, find, jnp.int32(0))

    def locate(d, begin):
        count = counts[d]
        within = jnp.bitwise_and(residue - begin, N_DEV - 1)

        @pl.when(within < count)
        def _():
            slot = lax.shift_right_logical(begin + within, 5)
            source[slot] = d
            live[slot] = 4 * groups[d * SRC_WIN + within]

        return begin + count

    lax.fori_loop(0, N_DEV, locate, jnp.int32(0))

    def window_copy(k):
        return pltpu.make_async_copy(
            arrived.at[source[k]], windows.at[pl.ds(k * WIN, WIN)], xsem.at[k]
        )

    def weight_copy(n, core, across):
        row = jnp.bitwise_xor(here, across) * HALF
        column = jnp.bitwise_xor(side, core) * CHUNK
        to = weights.at[
            place[3 + n],
            pl.ds(pl.multiple_of(row, HALF), HALF),
            pl.ds(pl.multiple_of(column, CHUNK), CHUNK),
        ]
        return pltpu.make_async_copy(pieces[8 * core + 2 * n + across], to, wsem.at[n, core, across])

    for k in range(DST_WIN):
        window_copy(k).start()
    for n in range(4):
        for core in range(2):
            for across in range(2):
                weight_copy(n, core, across).start()
    for k in range(DST_WIN):
        window_copy(k).wait()
        rows = pl.ds(k * WIN, WIN)
        values = windows[rows, :].astype(F32)
        mean = jnp.mean(values * values, axis=-1, keepdims=True)
        normed[rows, :] = (values * lax.rsqrt(mean + 1e-6) * norm_gain[...]).astype(BF16)

    for n in range(4):
        block = place[3 + n]
        for core in range(2):
            for across in range(2):
                weight_copy(n, core, across).wait()

        @pl.when(block < 3)
        def _(block=block):
            product = jnp.dot(normed[...], weights[block], preferred_element_type=F32)
            triple[block] = (product + qkv_bias[block]).astype(BF16)

    def attend(w, carry):
        rows = pl.ds(pl.multiple_of(w * WIN, WIN), WIN)
        dead = lax.broadcasted_iota(jnp.int32, (WIN, 2 * WIN), 0) >= live[w]
        zero = jnp.zeros((), BF16)
        for half in range(2):
            parts = [None] * (CHUNK // 128)
            for pair in range(HEADS // 4):
                begin = pair * 2 * HD
                low = begin // 128 * 128
                lane = low + lax.broadcasted_iota(jnp.int32, (WIN, 256), 1)
                first = (lane >= begin) & (lane < begin + HD)
                second = (lane >= begin + HD) & (lane < begin + 2 * HD)
                at = half * CHUNK + low
                q = triple[0, rows, at : at + 256]
                k = triple[1, rows, at : at + 256]
                v = triple[2, rows, at : at + 256]
                both = jnp.concatenate([jnp.where(first, q, zero), jnp.where(second, q, zero)], axis=0)
                scores = lax.dot_general(
                    k, both, (((1,), (1,)), ((), ())), preferred_element_type=F32
                )
                scores = jnp.where(dead, -1e30, scores)
                highest = jnp.max(scores, axis=0, keepdims=True)
                powers = jnp.exp2((scores - highest) * EXP2_SCALE)
                probs = powers * (1.0 / jnp.sum(powers, axis=0, keepdims=True))
                product = lax.dot_general(
                    probs.astype(BF16), v, (((0,), (0,)), ((), ())), preferred_element_type=F32
                )
                product = jnp.where(first, product[:WIN], jnp.where(second, product[WIN:], 0.0))
                for t in range(2):
                    tile, part = low // 128 + t, product[:, 128 * t : 128 * t + 128]
                    parts[tile] = part if parts[tile] is None else parts[tile] + part
            for tile in range(CHUNK // 128):
                at = half * CHUNK + tile * 128
                mixed[rows, at : at + 128] = parts[tile].astype(BF16)
        return carry

    lax.fori_loop(0, DST_WIN, attend, 0, unroll=True)

    encoded[...] = jnp.dot(mixed[...], weights[3], preferred_element_type=F32)
    for k in range(DST_WIN):
        rows = pl.ds(k * WIN, WIN)
        values = windows[rows, :].astype(F32) + encoded[rows, :] + proj_bias[...]
        mean = jnp.mean(values * values, axis=-1, keepdims=True)
        alive = lax.broadcasted_iota(jnp.int32, (WIN, 1), 0) < live[k]
        scale = jnp.where(alive, lax.rsqrt(mean + 1e-6), 0.0)
        values = values * scale * merge_gain[...]
        for t in range(D // 128):
            final[t, rows, :] = values[:, t * 128 : t * 128 + 128]

    at = lax.broadcasted_iota(jnp.int32, (MERGED, MERGED), 1)
    earlier = lax.broadcasted_iota(jnp.int32, (MERGED, MERGED), 0) < at
    same = owner_column[...] == owner_row[...]
    rank = jnp.sum(jnp.where(same & earlier, 1, 0), axis=0, keepdims=True)
    places = owner_row[...] * CAP + rank
    chosen = lax.broadcasted_iota(jnp.int32, (N_SEC * CAP, MERGED), 0) == places
    chosen = jnp.where(chosen, 1.0, 0.0).astype(BF16)
    for p in range(4):
        merged = [final[t, pl.ds(p, MERGED, stride=4), :] for t in range(D // 128)]
        merged = jnp.concatenate(merged, axis=1).astype(BF16)
        packed = jnp.dot(chosen, merged, preferred_element_type=F32)
        out[:, p * D : (p + 1) * D] = packed.astype(BF16)


def encode(place, counts, perm, groups, owner_row, owner_column, gain, qb, pb, mg, arrived, pieces):
    smem = pl.BlockSpec(memory_space=pltpu.SMEM)
    vmem = pl.BlockSpec(memory_space=pltpu.VMEM)
    hbm = pl.BlockSpec(memory_space=pl.ANY)
    return pl.pallas_call(
        encode_kernel,
        out_shape=jax.ShapeDtypeStruct((N_SEC * CAP, COLS), BF16),
        in_specs=[smem] * 4 + [vmem] * 6 + [hbm] * 17,
        out_specs=vmem,
        scratch_shapes=[
            pltpu.VMEM((4, D, D), BF16),
            pltpu.VMEM((ROWS, D), BF16),
            pltpu.VMEM((ROWS, D), BF16),
            pltpu.VMEM((3, ROWS, D), BF16),
            pltpu.VMEM((ROWS, D), BF16),
            pltpu.VMEM((ROWS, D), F32),
            pltpu.VMEM((D // 128, ROWS, 128), F32),
            pltpu.SMEM((DST_WIN,), jnp.int32),
            pltpu.SMEM((DST_WIN,), jnp.int32),
            pltpu.SemaphoreType.DMA((4, 2, 2)),
            pltpu.SemaphoreType.DMA((DST_WIN,)),
        ],
        compiler_params=pltpu.CompilerParams(vmem_limit_bytes=VMEM_LIMIT),
        name="encode",
    )(place, counts, perm, groups, owner_row, owner_column, gain, qb, pb, mg, arrived, *pieces)


def shift(n, k):
    return [(i, (i + k) % n) for i in range(n)]


SWAP = [(0, 1), (1, 0)]
CROSS = [(i, 3 - i) for i in range(4)]
CROSS3 = [(i, 7 - i) for i in range(8)]


def gather_weights(qkv_weight, proj_weight):
    y, xl, c = lax.axis_index("y"), lax.axis_index("xl"), lax.axis_index("c")
    send = lax.ppermute
    side = jnp.bitwise_xor(xl, c)
    chunk = 2 * y + side
    from_qkv = lax.dynamic_slice(qkv_weight, (0, jnp.minimum(chunk, 5) * CHUNK), (40, CHUNK))
    from_proj = lax.dynamic_slice(proj_weight, (0, jnp.maximum(chunk - 6, 0) * CHUNK), (40, CHUNK))
    own = jnp.where(chunk < 6, from_qkv, from_proj)
    column = lax.all_to_all(jnp.broadcast_to(own[None], (8, 40, CHUNK)), "z", 0, 0, tiled=True)
    return column, side


def spread_weights(column, side):
    y, xh, c = lax.axis_index("y"), lax.axis_index("xh"), lax.axis_index("c")
    send = lax.ppermute
    partner = send(column, ("xl", "c"), CROSS)
    low, high = jnp.where(c == 0, column, partner), jnp.where(c == 0, partner, column)
    here = jnp.concatenate([low, high], axis=1).reshape(HALF, CHUNK)
    across = send(here, ("xl", "xh", "c"), CROSS3)
    up_h, down_h = send(here, "y", shift(4, 1)), send(here, "y", shift(4, -1))
    up_a, down_a = send(across, "y", shift(4, 1)), send(across, "y", shift(4, -1))
    far_h, far_a = send(up_h, "y", shift(4, 1)), send(down_a, "y", shift(4, -1))
    pieces = [here, across, up_h, up_a, down_h, down_a, far_h, far_a]
    pieces = pieces + [send(p, "c", SWAP) for p in pieces]
    return pieces, [xh, side] + [jnp.mod(y - step, 4) for step in (0, 1, -1, 2)]


def body(
    patches,
    win_count,
    dest_perm,
    win_groups,
    norm_gain,
    qkv_weight,
    qkv_bias,
    proj_weight,
    proj_bias,
    merge_gain,
    owner,
):
    position = lax.axis_index(("xh", "z", "c"))
    counts, perm = win_count[0], dest_perm[0]
    column, side = gather_weights(qkv_weight, proj_weight)
    going = outgoing(
        position.astype(jnp.int32).reshape(1), counts, perm, patches.reshape(SRC_WIN, WIN, D)
    )
    pieces, placed = spread_weights(column, side)
    place = jnp.stack([position] + placed).astype(jnp.int32)
    arrived = lax.all_to_all(going, ("xh", "z", "c"), split_axis=0, concat_axis=0, tiled=True)
    packed = encode(
        place,
        counts,
        perm,
        win_groups.reshape(N_DEV * SRC_WIN),
        owner.reshape(1, MERGED),
        owner.reshape(MERGED, 1),
        norm_gain.reshape(1, D),
        qkv_bias.reshape(3, 1, D),
        proj_bias.reshape(1, D),
        merge_gain.reshape(1, D),
        arrived,
        pieces,
    )
    delivered = lax.all_to_all(packed, ("y", "xl"), split_axis=0, concat_axis=0, tiled=True)
    return delivered.reshape(1, N_SEC * CAP, COLS)


def solution(mesh):
    fine = Mesh(mesh.devices.reshape(4, 2, 2, 8, 2), ("y", "xl", "xh", "z", "c"))
    sec, dev = ("y", "xl"), ("xh", "z", "c")
    return jax.shard_map(
        body,
        mesh=fine,
        in_specs=(
            P(sec, dev, None),
            P(sec, None),
            P(sec, None),
            P(sec, None, None),
            P(),
            P(dev, None),
            P(),
            P(dev, None),
            P(),
            P(),
            P(sec, dev, None),
        ),
        out_specs=P(sec, dev, None),
        check_vma=False,
    )
```

```python
import math

import jax
import jax.numpy as jnp
from jax import lax
from jax.experimental import pallas as pl
from jax.experimental.pallas import tpu as pltpu
from jax.sharding import Mesh
from jax.sharding import PartitionSpec as P

D = 1280
HEADS = 16
HD = 80
WIN = 64
DST_WIN = 8
SRC_WIN = 24
N_DEV = 32
N_SEC = 8
CAP = 32
ROWS = DST_WIN * WIN
MERGED = ROWS // 4
COLS = 4 * D
CHUNK = 640
HALF = 640
PART = 320
PIECES = 9
EXP2_SCALE = HD ** (-0.5) * math.log2(math.e)
VMEM_LIMIT = 48 * 1024 * 1024

F32 = jnp.float32
BF16 = jnp.bfloat16


def outgoing_kernel(place, counts, perm, groups, patches, out, table, staged, in_sem, out_sem):
    pos = place[0]
    mine = counts[pos]

    def load(i):
        return pltpu.make_async_copy(patches.at[i], staged.at[i], in_sem.at[i])

    for i in range(SRC_WIN):

        @pl.when(i < mine)
        def _(i=i):
            load(i).start()

    def add(d, total):
        return total + jnp.where(d < pos, counts[d], 0)

    begin = lax.fori_loop(0, N_DEV, add, jnp.int32(0))

    def save(i):
        slot = perm[jnp.bitwise_and(begin + i, N_DEV - 1)]
        return pltpu.make_async_copy(staged.at[i], out.at[slot], out_sem.at[i])

    for i in range(SRC_WIN):

        @pl.when(i < mine)
        def _(i=i):
            load(i).wait()
            save(i).start()

    def find(r, found):
        return jnp.where(perm[r] == pos, r, found)

    residue = lax.fori_loop(0, N_DEV, find, jnp.int32(0))

    def locate(d, before):
        count = counts[d]
        within = jnp.bitwise_and(residue - before, N_DEV - 1)

        @pl.when(within < count)
        def _():
            slot = lax.shift_right_logical(before + within, 5)
            table[slot] = d
            table[DST_WIN + slot] = 4 * groups[d * SRC_WIN + within]

        return before + count

    lax.fori_loop(0, N_DEV, locate, jnp.int32(0))

    for i in range(SRC_WIN):

        @pl.when(i < mine)
        def _(i=i):
            save(i).wait()


def outgoing(place, counts, perm, groups, patches):
    smem = pl.BlockSpec(memory_space=pltpu.SMEM)
    return pl.pallas_call(
        outgoing_kernel,
        out_shape=(
            jax.ShapeDtypeStruct((N_DEV, WIN, D), patches.dtype),
            jax.ShapeDtypeStruct((2 * DST_WIN,), jnp.int32),
        ),
        in_specs=[smem, smem, smem, smem, pl.BlockSpec(memory_space=pltpu.HBM)],
        out_specs=(pl.BlockSpec(memory_space=pltpu.HBM), smem),
        scratch_shapes=[
            pltpu.VMEM((SRC_WIN, WIN, D), patches.dtype),
            pltpu.SemaphoreType.DMA((SRC_WIN,)),
            pltpu.SemaphoreType.DMA((SRC_WIN,)),
        ],
        compiler_params=pltpu.CompilerParams(vmem_limit_bytes=60 * 1024 * 1024),
        name="outgoing",
    )(place, counts, perm, groups, patches)


def encode_kernel(
    place,
    table,
    owner_row,
    owner_column,
    norm_gain,
    qkv_bias,
    proj_bias,
    merge_gain,
    arrived,
    *rest,
):
    pieces = rest[: 2 * PIECES]
    out, weights, windows, normed, triple, mixed, encoded, final, wsem, xsem = rest[2 * PIECES :]
    here, side = place[0], place[1]

    def window_copy(k):
        return pltpu.make_async_copy(
            arrived.at[table[k]], windows.at[pl.ds(k * WIN, WIN)], xsem.at[k]
        )

    def weight_copy(core, piece):
        n, across = min(piece // 2, 3), min(piece % 2 + piece // 8, 1)
        rows = PART if piece >= 7 else HALF
        row = jnp.bitwise_xor(here, across) * HALF + (PART if piece == 8 else 0)
        column = jnp.bitwise_xor(side, core) * CHUNK
        to = weights.at[
            place[2 + n],
            pl.ds(pl.multiple_of(row, PART), rows),
            pl.ds(pl.multiple_of(column, CHUNK), CHUNK),
        ]
        return pltpu.make_async_copy(pieces[PIECES * core + piece], to, wsem.at[core, piece])

    def block_copies(n):
        return [weight_copy(core, p) for core in range(2) for p in ((2 * n, 2 * n + 1) if n < 3 else (6, 7, 8))]

    for k in range(DST_WIN):
        window_copy(k).start()
    for n in range(4):
        for copy in block_copies(n):
            copy.start()
    for k in range(DST_WIN):
        window_copy(k).wait()
        rows = pl.ds(k * WIN, WIN)
        values = windows[rows, :].astype(F32)
        mean = jnp.mean(values * values, axis=-1, keepdims=True)
        normed[rows, :] = (values * lax.rsqrt(mean + 1e-6) * norm_gain[...]).astype(BF16)

    for n in range(4):
        block = place[2 + n]
        for copy in block_copies(n):
            copy.wait()

        @pl.when(block < 3)
        def _(block=block):
            product = jnp.dot(normed[...], weights[block], preferred_element_type=F32)
            triple[block] = (product + qkv_bias[block]).astype(BF16)

    def attend(w, carry):
        rows = pl.ds(pl.multiple_of(w * WIN, WIN), WIN)
        dead = lax.broadcasted_iota(jnp.int32, (WIN, 2 * WIN), 0) >= table[DST_WIN + w]
        zero = jnp.zeros((), BF16)
        for half in range(2):
            parts = [None] * (CHUNK // 128)
            for pair in range(HEADS // 4):
                begin = pair * 2 * HD
                low = begin // 128 * 128
                lane = low + lax.broadcasted_iota(jnp.int32, (WIN, 256), 1)
                first = (lane >= begin) & (lane < begin + HD)
                second = (lane >= begin + HD) & (lane < begin + 2 * HD)
                at = half * CHUNK + low
                q = triple[0, rows, at : at + 256]
                k = triple[1, rows, at : at + 256]
                v = triple[2, rows, at : at + 256]
                both = jnp.concatenate([jnp.where(first, q, zero), jnp.where(second, q, zero)], axis=0)
                scores = lax.dot_general(
                    k, both, (((1,), (1,)), ((), ())), preferred_element_type=F32
                )
                scores = jnp.where(dead, -1e30, scores)
                highest = jnp.max(scores, axis=0, keepdims=True)
                powers = jnp.exp2((scores - highest) * EXP2_SCALE)
                probs = powers * (1.0 / jnp.sum(powers, axis=0, keepdims=True))
                product = lax.dot_general(
                    probs.astype(BF16), v, (((0,), (0,)), ((), ())), preferred_element_type=F32
                )
                product = jnp.where(first, product[:WIN], jnp.where(second, product[WIN:], 0.0))
                for t in range(2):
                    tile, part = low // 128 + t, product[:, 128 * t : 128 * t + 128]
                    parts[tile] = part if parts[tile] is None else parts[tile] + part
            for tile in range(CHUNK // 128):
                at = half * CHUNK + tile * 128
                mixed[rows, at : at + 128] = parts[tile].astype(BF16)
        return carry

    lax.fori_loop(0, DST_WIN, attend, 0, unroll=True)

    encoded[...] = jnp.dot(mixed[...], weights[3], preferred_element_type=F32)
    for k in range(DST_WIN):
        rows = pl.ds(k * WIN, WIN)
        values = windows[rows, :].astype(F32) + encoded[rows, :] + proj_bias[...]
        mean = jnp.mean(values * values, axis=-1, keepdims=True)
        alive = lax.broadcasted_iota(jnp.int32, (WIN, 1), 0) < table[DST_WIN + k]
        scale = jnp.where(alive, lax.rsqrt(mean + 1e-6), 0.0)
        values = values * scale * merge_gain[...]
        for t in range(D // 128):
            final[t, rows, :] = values[:, t * 128 : t * 128 + 128]

    at = lax.broadcasted_iota(jnp.int32, (MERGED, MERGED), 1)
    earlier = lax.broadcasted_iota(jnp.int32, (MERGED, MERGED), 0) < at
    same = owner_column[...] == owner_row[...]
    rank = jnp.sum(jnp.where(same & earlier, 1, 0), axis=0, keepdims=True)
    places = owner_row[...] * CAP + rank
    chosen = lax.broadcasted_iota(jnp.int32, (N_SEC * CAP, MERGED), 0) == places
    chosen = jnp.where(chosen, 1.0, 0.0).astype(BF16)
    for p in range(4):
        merged = [final[t, pl.ds(p, MERGED, stride=4), :] for t in range(D // 128)]
        merged = jnp.concatenate(merged, axis=1).astype(BF16)
        packed = jnp.dot(chosen, merged, preferred_element_type=F32)
        out[:, p * D : (p + 1) * D] = packed.astype(BF16)


def encode(place, table, owner_row, owner_column, gain, qb, pb, mg, arrived, pieces):
    smem = pl.BlockSpec(memory_space=pltpu.SMEM)
    vmem = pl.BlockSpec(memory_space=pltpu.VMEM)
    hbm = pl.BlockSpec(memory_space=pl.ANY)
    return pl.pallas_call(
        encode_kernel,
        out_shape=jax.ShapeDtypeStruct((N_SEC * CAP, COLS), BF16),
        in_specs=[smem] * 2 + [vmem] * 6 + [hbm] * (1 + 2 * PIECES),
        out_specs=vmem,
        scratch_shapes=[
            pltpu.VMEM((4, D, D), BF16),
            pltpu.VMEM((ROWS, D), BF16),
            pltpu.VMEM((ROWS, D), BF16),
            pltpu.VMEM((3, ROWS, D), BF16),
            pltpu.VMEM((ROWS, D), BF16),
            pltpu.VMEM((ROWS, D), F32),
            pltpu.VMEM((D // 128, ROWS, 128), F32),
            pltpu.SemaphoreType.DMA((2, PIECES)),
            pltpu.SemaphoreType.DMA((DST_WIN,)),
        ],
        compiler_params=pltpu.CompilerParams(vmem_limit_bytes=VMEM_LIMIT),
        name="encode",
    )(place, table, owner_row, owner_column, gain, qb, pb, mg, arrived, *pieces)


def shift(n, k):
    return [(i, (i + k) % n) for i in range(n)]


SWAP = [(0, 1), (1, 0)]
CROSS = [(i, 3 - i) for i in range(4)]
CROSS3 = [(i, 7 - i) for i in range(8)]


def gather_weights(qkv_weight, proj_weight):
    y, xl, c = lax.axis_index("y"), lax.axis_index("xl"), lax.axis_index("c")
    send = lax.ppermute
    side = jnp.bitwise_xor(xl, c)
    chunk = 2 * y + side
    from_qkv = lax.dynamic_slice(qkv_weight, (0, jnp.minimum(chunk, 5) * CHUNK), (40, CHUNK))
    from_proj = lax.dynamic_slice(proj_weight, (0, jnp.maximum(chunk - 6, 0) * CHUNK), (40, CHUNK))
    own = jnp.where(chunk < 6, from_qkv, from_proj)
    column = lax.all_to_all(jnp.broadcast_to(own[None], (8, 40, CHUNK)), "z", 0, 0, tiled=True)
    return column, side


def spread_weights(column, side):
    y, xh, c = lax.axis_index("y"), lax.axis_index("xh"), lax.axis_index("c")
    send = lax.ppermute
    partner = send(column, ("xl", "c"), CROSS)
    low, high = jnp.where(c == 0, column, partner), jnp.where(c == 0, partner, column)
    here = jnp.concatenate([low, high], axis=1).reshape(HALF, CHUNK)
    across = send(here, ("xl", "xh", "c"), CROSS3)
    up_h, down_h = send(here, "y", shift(4, 1)), send(here, "y", shift(4, -1))
    up_a, down_a = send(across, "y", shift(4, 1)), send(across, "y", shift(4, -1))
    far_h = send(up_h, "y", shift(4, 1))
    far_low, far_high = send(up_a[:PART], "y", shift(4, 1)), send(down_a[PART:], "y", shift(4, -1))
    pieces = [here, across, up_h, up_a, down_h, down_a, far_h, far_low, far_high]
    pieces = pieces + [send(p, "c", SWAP) for p in pieces]
    return pieces, [xh, side] + [jnp.mod(y - step, 4) for step in (0, 1, -1, 2)]


def body(
    patches,
    win_count,
    dest_perm,
    win_groups,
    norm_gain,
    qkv_weight,
    qkv_bias,
    proj_weight,
    proj_bias,
    merge_gain,
    owner,
):
    position = lax.axis_index(("xh", "z", "c"))
    counts, perm = win_count[0], dest_perm[0]
    column, side = gather_weights(qkv_weight, proj_weight)
    going, table = outgoing(
        position.astype(jnp.int32).reshape(1),
        counts,
        perm,
        win_groups.reshape(N_DEV * SRC_WIN),
        patches.reshape(SRC_WIN, WIN, D),
    )
    pieces, placed = spread_weights(column, side)
    place = jnp.stack(placed).astype(jnp.int32)
    arrived = lax.all_to_all(going, ("xh", "z", "c"), split_axis=0, concat_axis=0, tiled=True)
    packed = encode(
        place,
        table,
        owner.reshape(1, MERGED),
        owner.reshape(MERGED, 1),
        norm_gain.reshape(1, D),
        qkv_bias.reshape(3, 1, D),
        proj_bias.reshape(1, D),
        merge_gain.reshape(1, D),
        arrived,
        pieces,
    )
    delivered = lax.all_to_all(packed, ("y", "xl"), split_axis=0, concat_axis=0, tiled=True)
    return delivered.reshape(1, N_SEC * CAP, COLS)


def solution(mesh):
    fine = Mesh(mesh.devices.reshape(4, 2, 2, 8, 2), ("y", "xl", "xh", "z", "c"))
    sec, dev = ("y", "xl"), ("xh", "z", "c")
    return jax.shard_map(
        body,
        mesh=fine,
        in_specs=(
            P(sec, dev, None),
            P(sec, None),
            P(sec, None),
            P(sec, None, None),
            P(),
            P(dev, None),
            P(),
            P(dev, None),
            P(),
            P(),
            P(sec, dev, None),
        ),
        out_specs=P(sec, dev, None),
        check_vma=False,
    )
```

```python
import math

import jax
import jax.numpy as jnp
from jax import lax
from jax.experimental import pallas as pl
from jax.experimental.pallas import tpu as pltpu
from jax.sharding import Mesh
from jax.sharding import PartitionSpec as P

D = 1280
HEADS = 16
HD = 80
WIN = 64
DST_WIN = 8
SRC_WIN = 24
N_DEV = 32
N_SEC = 8
CAP = 32
ROWS = DST_WIN * WIN
MERGED = ROWS // 4
COLS = 4 * D
CHUNK = 640
HALF = 640
EXP2_SCALE = HD ** (-0.5) * math.log2(math.e)
VMEM_LIMIT = 48 * 1024 * 1024

F32 = jnp.float32
BF16 = jnp.bfloat16


def outgoing_kernel(place, counts, perm, groups, patches, out, table, staged, in_sem, out_sem):
    pos = place[0]
    mine = counts[pos]

    def load(i):
        return pltpu.make_async_copy(patches.at[i], staged.at[i], in_sem.at[i])

    for i in range(SRC_WIN):

        @pl.when(i < mine)
        def _(i=i):
            load(i).start()

    def add(d, total):
        return total + jnp.where(d < pos, counts[d], 0)

    begin = lax.fori_loop(0, N_DEV, add, jnp.int32(0))

    def save(i):
        slot = perm[jnp.bitwise_and(begin + i, N_DEV - 1)]
        return pltpu.make_async_copy(staged.at[i], out.at[slot], out_sem.at[i])

    for i in range(SRC_WIN):

        @pl.when(i < mine)
        def _(i=i):
            load(i).wait()
            save(i).start()

    def find(r, found):
        return jnp.where(perm[r] == pos, r, found)

    residue = lax.fori_loop(0, N_DEV, find, jnp.int32(0))

    def locate(d, before):
        count = counts[d]
        within = jnp.bitwise_and(residue - before, N_DEV - 1)

        @pl.when(within < count)
        def _():
            slot = lax.shift_right_logical(before + within, 5)
            table[slot] = d
            table[DST_WIN + slot] = 4 * groups[d * SRC_WIN + within]

        return before + count

    lax.fori_loop(0, N_DEV, locate, jnp.int32(0))

    for i in range(SRC_WIN):

        @pl.when(i < mine)
        def _(i=i):
            save(i).wait()


def outgoing(place, counts, perm, groups, patches):
    smem = pl.BlockSpec(memory_space=pltpu.SMEM)
    return pl.pallas_call(
        outgoing_kernel,
        out_shape=(
            jax.ShapeDtypeStruct((N_DEV, WIN, D), patches.dtype),
            jax.ShapeDtypeStruct((2 * DST_WIN,), jnp.int32),
        ),
        in_specs=[smem, smem, smem, smem, pl.BlockSpec(memory_space=pltpu.HBM)],
        out_specs=(pl.BlockSpec(memory_space=pltpu.HBM), smem),
        scratch_shapes=[
            pltpu.VMEM((SRC_WIN, WIN, D), patches.dtype),
            pltpu.SemaphoreType.DMA((SRC_WIN,)),
            pltpu.SemaphoreType.DMA((SRC_WIN,)),
        ],
        compiler_params=pltpu.CompilerParams(vmem_limit_bytes=60 * 1024 * 1024),
        name="outgoing",
    )(place, counts, perm, groups, patches)


def encode_kernel(
    place,
    table,
    owner_row,
    owner_column,
    norm_gain,
    qkv_bias,
    proj_bias,
    merge_gain,
    arrived,
    *rest,
):
    pieces = rest[:16]
    out, weights, windows, normed, triple, mixed, encoded, final, wsem, xsem = rest[16:]
    here, side = place[0], place[1]

    def window_copy(k):
        return pltpu.make_async_copy(
            arrived.at[table[k]], windows.at[pl.ds(k * WIN, WIN)], xsem.at[k]
        )

    def weight_copy(n, core, across):
        row = jnp.bitwise_xor(here, across) * HALF
        column = jnp.bitwise_xor(side, core) * CHUNK
        to = weights.at[
            place[2 + n],
            pl.ds(pl.multiple_of(row, HALF), HALF),
            pl.ds(pl.multiple_of(column, CHUNK), CHUNK),
        ]
        return pltpu.make_async_copy(pieces[8 * core + 2 * n + across], to, wsem.at[n, core, across])

    for k in range(DST_WIN):
        window_copy(k).start()
    for n in range(4):
        for core in range(2):
            for across in range(2):
                weight_copy(n, core, across).start()
    for k in range(DST_WIN):
        window_copy(k).wait()
        rows = pl.ds(k * WIN, WIN)
        values = windows[rows, :].astype(F32)
        mean = jnp.mean(values * values, axis=-1, keepdims=True)
        normed[rows, :] = (values * lax.rsqrt(mean + 1e-6) * norm_gain[...]).astype(BF16)

    for n in range(4):
        block = place[2 + n]
        for core in range(2):
            for across in range(2):
                weight_copy(n, core, across).wait()

        @pl.when(block < 3)
        def _(block=block):
            product = jnp.dot(normed[...], weights[block], preferred_element_type=F32)
            triple[block] = (product + qkv_bias[block]).astype(BF16)

    def attend(w, carry):
        rows = pl.ds(pl.multiple_of(w * WIN, WIN), WIN)
        dead = lax.broadcasted_iota(jnp.int32, (WIN, 2 * WIN), 0) >= table[DST_WIN + w]
        zero = jnp.zeros((), BF16)
        for half in range(2):
            parts = [None] * (CHUNK // 128)
            for pair in range(HEADS // 4):
                begin = pair * 2 * HD
                low = begin // 128 * 128
                lane = low + lax.broadcasted_iota(jnp.int32, (WIN, 256), 1)
                first = (lane >= begin) & (lane < begin + HD)
                second = (lane >= begin + HD) & (lane < begin + 2 * HD)
                at = half * CHUNK + low
                q = triple[0, rows, at : at + 256]
                k = triple[1, rows, at : at + 256]
                v = triple[2, rows, at : at + 256]
                both = jnp.concatenate([jnp.where(first, q, zero), jnp.where(second, q, zero)], axis=0)
                scores = lax.dot_general(
                    k, both, (((1,), (1,)), ((), ())), preferred_element_type=F32
                )
                scores = jnp.where(dead, -1e30, scores)
                highest = jnp.max(scores, axis=0, keepdims=True)
                powers = jnp.exp2((scores - highest) * EXP2_SCALE)
                probs = powers * (1.0 / jnp.sum(powers, axis=0, keepdims=True))
                product = lax.dot_general(
                    probs.astype(BF16), v, (((0,), (0,)), ((), ())), preferred_element_type=F32
                )
                product = jnp.where(first, product[:WIN], jnp.where(second, product[WIN:], 0.0))
                for t in range(2):
                    tile, part = low // 128 + t, product[:, 128 * t : 128 * t + 128]
                    parts[tile] = part if parts[tile] is None else parts[tile] + part
            for tile in range(CHUNK // 128):
                at = half * CHUNK + tile * 128
                mixed[rows, at : at + 128] = parts[tile].astype(BF16)
        return carry

    lax.fori_loop(0, DST_WIN, attend, 0, unroll=True)

    encoded[...] = jnp.dot(mixed[...], weights[3], preferred_element_type=F32)
    for k in range(DST_WIN):
        rows = pl.ds(k * WIN, WIN)
        values = windows[rows, :].astype(F32) + encoded[rows, :] + proj_bias[...]
        mean = jnp.mean(values * values, axis=-1, keepdims=True)
        alive = lax.broadcasted_iota(jnp.int32, (WIN, 1), 0) < table[DST_WIN + k]
        scale = jnp.where(alive, lax.rsqrt(mean + 1e-6), 0.0)
        values = values * scale * merge_gain[...]
        for t in range(D // 128):
            final[t, rows, :] = values[:, t * 128 : t * 128 + 128]

    at = lax.broadcasted_iota(jnp.int32, (MERGED, MERGED), 1)
    earlier = lax.broadcasted_iota(jnp.int32, (MERGED, MERGED), 0) < at
    same = owner_column[...] == owner_row[...]
    rank = jnp.sum(jnp.where(same & earlier, 1, 0), axis=0, keepdims=True)
    places = owner_row[...] * CAP + rank
    chosen = lax.broadcasted_iota(jnp.int32, (N_SEC * CAP, MERGED), 0) == places
    chosen = jnp.where(chosen, 1.0, 0.0).astype(BF16)
    for p in range(4):
        merged = [final[t, pl.ds(p, MERGED, stride=4), :] for t in range(D // 128)]
        merged = jnp.concatenate(merged, axis=1).astype(BF16)
        packed = jnp.dot(chosen, merged, preferred_element_type=F32)
        out[:, p * D : (p + 1) * D] = packed.astype(BF16)


def encode(place, table, owner_row, owner_column, gain, qb, pb, mg, arrived, pieces):
    smem = pl.BlockSpec(memory_space=pltpu.SMEM)
    vmem = pl.BlockSpec(memory_space=pltpu.VMEM)
    hbm = pl.BlockSpec(memory_space=pl.ANY)
    return pl.pallas_call(
        encode_kernel,
        out_shape=jax.ShapeDtypeStruct((N_SEC * CAP, COLS), BF16),
        in_specs=[smem] * 2 + [vmem] * 6 + [hbm] * 17,
        out_specs=vmem,
        scratch_shapes=[
            pltpu.VMEM((4, D, D), BF16),
            pltpu.VMEM((ROWS, D), BF16),
            pltpu.VMEM((ROWS, D), BF16),
            pltpu.VMEM((3, ROWS, D), BF16),
            pltpu.VMEM((ROWS, D), BF16),
            pltpu.VMEM((ROWS, D), F32),
            pltpu.VMEM((D // 128, ROWS, 128), F32),
            pltpu.SemaphoreType.DMA((4, 2, 2)),
            pltpu.SemaphoreType.DMA((DST_WIN,)),
        ],
        compiler_params=pltpu.CompilerParams(vmem_limit_bytes=VMEM_LIMIT),
        name="encode",
    )(place, table, owner_row, owner_column, gain, qb, pb, mg, arrived, *pieces)


def shift(n, k):
    return [(i, (i + k) % n) for i in range(n)]


SWAP = [(0, 1), (1, 0)]
CROSS = [(i, 3 - i) for i in range(4)]
CROSS3 = [(i, 7 - i) for i in range(8)]


def gather_weights(qkv_weight, proj_weight):
    y, xl, c = lax.axis_index("y"), lax.axis_index("xl"), lax.axis_index("c")
    send = lax.ppermute
    side = jnp.bitwise_xor(xl, c)
    chunk = 2 * y + side
    from_qkv = lax.dynamic_slice(qkv_weight, (0, jnp.minimum(chunk, 5) * CHUNK), (40, CHUNK))
    from_proj = lax.dynamic_slice(proj_weight, (0, jnp.maximum(chunk - 6, 0) * CHUNK), (40, CHUNK))
    own = jnp.where(chunk < 6, from_qkv, from_proj)
    column = lax.all_to_all(jnp.broadcast_to(own[None], (8, 40, CHUNK)), "z", 0, 0, tiled=True)
    return column, side


def spread_weights(column, side):
    y, xh, c = lax.axis_index("y"), lax.axis_index("xh"), lax.axis_index("c")
    send = lax.ppermute
    partner = send(column, ("xl", "c"), CROSS)
    across_column = send(column, ("xl", "xh", "c"), CROSS3)
    across_partner = send(partner, ("xl", "xh", "c"), CROSS3)

    def joined(even, odd):
        low, high = jnp.where(c == 0, even, odd), jnp.where(c == 0, odd, even)
        return jnp.concatenate([low, high], axis=1).reshape(HALF, CHUNK)

    here, across = joined(column, partner), joined(across_partner, across_column)
    up_h, down_h = send(here, "y", shift(4, 1)), send(here, "y", shift(4, -1))
    up_a, down_a = send(across, "y", shift(4, 1)), send(across, "y", shift(4, -1))
    far_h, far_a = send(up_h, "y", shift(4, 1)), send(down_a, "y", shift(4, -1))
    pieces = [here, across, up_h, up_a, down_h, down_a, far_h, far_a]
    pieces = pieces + [send(p, "c", SWAP) for p in pieces]
    return pieces, [xh, side] + [jnp.mod(y - step, 4) for step in (0, 1, -1, 2)]


def body(
    patches,
    win_count,
    dest_perm,
    win_groups,
    norm_gain,
    qkv_weight,
    qkv_bias,
    proj_weight,
    proj_bias,
    merge_gain,
    owner,
):
    position = lax.axis_index(("xh", "z", "c"))
    counts, perm = win_count[0], dest_perm[0]
    column, side = gather_weights(qkv_weight, proj_weight)
    going, table = outgoing(
        position.astype(jnp.int32).reshape(1),
        counts,
        perm,
        win_groups.reshape(N_DEV * SRC_WIN),
        patches.reshape(SRC_WIN, WIN, D),
    )
    pieces, placed = spread_weights(column, side)
    place = jnp.stack(placed).astype(jnp.int32)
    arrived = lax.all_to_all(going, ("xh", "z", "c"), split_axis=0, concat_axis=0, tiled=True)
    packed = encode(
        place,
        table,
        owner.reshape(1, MERGED),
        owner.reshape(MERGED, 1),
        norm_gain.reshape(1, D),
        qkv_bias.reshape(3, 1, D),
        proj_bias.reshape(1, D),
        merge_gain.reshape(1, D),
        arrived,
        pieces,
    )
    delivered = lax.all_to_all(packed, ("y", "xl"), split_axis=0, concat_axis=0, tiled=True)
    return delivered.reshape(1, N_SEC * CAP, COLS)


def solution(mesh):
    fine = Mesh(mesh.devices.reshape(4, 2, 2, 8, 2), ("y", "xl", "xh", "z", "c"))
    sec, dev = ("y", "xl"), ("xh", "z", "c")
    return jax.shard_map(
        body,
        mesh=fine,
        in_specs=(
            P(sec, dev, None),
            P(sec, None),
            P(sec, None),
            P(sec, None, None),
            P(),
            P(dev, None),
            P(),
            P(dev, None),
            P(),
            P(),
            P(sec, dev, None),
        ),
        out_specs=P(sec, dev, None),
        check_vma=False,
    )
```

```python
import math

import jax
import jax.numpy as jnp
from jax import lax
from jax.experimental import pallas as pl
from jax.experimental.pallas import tpu as pltpu
from jax.sharding import Mesh
from jax.sharding import PartitionSpec as P

D = 1280
HEADS = 16
HD = 80
WIN = 64
DST_WIN = 8
SRC_WIN = 24
N_DEV = 32
N_SEC = 8
CAP = 32
ROWS = DST_WIN * WIN
MERGED = ROWS // 4
COLS = 4 * D
CHUNK = 640
HALF = 640
EXP2_SCALE = HD ** (-0.5) * math.log2(math.e)
VMEM_LIMIT = 48 * 1024 * 1024

F32 = jnp.float32
BF16 = jnp.bfloat16


def outgoing_kernel(place, counts, perm, groups, patches, out, table, staged, in_sem, out_sem):
    pos = place[0]
    mine = counts[pos]

    def load(i):
        return pltpu.make_async_copy(patches.at[i], staged.at[i], in_sem.at[i])

    for i in range(SRC_WIN):

        @pl.when(i < mine)
        def _(i=i):
            load(i).start()

    def add(d, total):
        return total + jnp.where(d < pos, counts[d], 0)

    begin = lax.fori_loop(0, N_DEV, add, jnp.int32(0))

    def save(i):
        slot = perm[jnp.bitwise_and(begin + i, N_DEV - 1)]
        return pltpu.make_async_copy(staged.at[i], out.at[slot], out_sem.at[i])

    for i in range(SRC_WIN):

        @pl.when(i < mine)
        def _(i=i):
            load(i).wait()
            save(i).start()

    def find(r, found):
        return jnp.where(perm[r] == pos, r, found)

    residue = lax.fori_loop(0, N_DEV, find, jnp.int32(0))

    def locate(d, before):
        count = counts[d]
        within = jnp.bitwise_and(residue - before, N_DEV - 1)

        @pl.when(within < count)
        def _():
            slot = lax.shift_right_logical(before + within, 5)
            table[slot] = d
            table[DST_WIN + slot] = 4 * groups[d * SRC_WIN + within]

        return before + count

    lax.fori_loop(0, N_DEV, locate, jnp.int32(0))

    for i in range(SRC_WIN):

        @pl.when(i < mine)
        def _(i=i):
            save(i).wait()


def outgoing(place, counts, perm, groups, patches):
    smem = pl.BlockSpec(memory_space=pltpu.SMEM)
    return pl.pallas_call(
        outgoing_kernel,
        out_shape=(
            jax.ShapeDtypeStruct((N_DEV, WIN, D), patches.dtype),
            jax.ShapeDtypeStruct((2 * DST_WIN,), jnp.int32),
        ),
        in_specs=[smem, smem, smem, smem, pl.BlockSpec(memory_space=pltpu.HBM)],
        out_specs=(pl.BlockSpec(memory_space=pltpu.HBM), smem),
        scratch_shapes=[
            pltpu.VMEM((SRC_WIN, WIN, D), patches.dtype),
            pltpu.SemaphoreType.DMA((SRC_WIN,)),
            pltpu.SemaphoreType.DMA((SRC_WIN,)),
        ],
        compiler_params=pltpu.CompilerParams(vmem_limit_bytes=60 * 1024 * 1024),
        name="outgoing",
    )(place, counts, perm, groups, patches)


def encode_kernel(
    place,
    table,
    owner_row,
    owner_column,
    norm_gain,
    qkv_bias,
    proj_bias,
    merge_gain,
    arrived,
    *rest,
):
    pieces = rest[:16]
    packed_rows, out, psem, weights, windows, normed, triple, mixed, encoded, final, wsem, xsem = rest[16:]
    here, side = place[0], place[1]

    def window_copy(k):
        return pltpu.make_async_copy(
            arrived.at[table[k]], windows.at[pl.ds(k * WIN, WIN)], xsem.at[k]
        )

    def weight_copy(n, core, across):
        row = jnp.bitwise_xor(here, across) * HALF
        column = jnp.bitwise_xor(side, core) * CHUNK
        to = weights.at[
            place[2 + n],
            pl.ds(pl.multiple_of(row, HALF), HALF),
            pl.ds(pl.multiple_of(column, CHUNK), CHUNK),
        ]
        return pltpu.make_async_copy(pieces[8 * core + 2 * n + across], to, wsem.at[n, core, across])

    for k in range(DST_WIN):
        window_copy(k).start()
    for n in range(4):
        for core in range(2):
            for across in range(2):
                weight_copy(n, core, across).start()
    for k in range(DST_WIN):
        window_copy(k).wait()
        rows = pl.ds(k * WIN, WIN)
        values = windows[rows, :].astype(F32)
        mean = jnp.mean(values * values, axis=-1, keepdims=True)
        normed[rows, :] = (values * lax.rsqrt(mean + 1e-6) * norm_gain[...]).astype(BF16)

    for n in range(4):
        block = place[2 + n]
        for core in range(2):
            for across in range(2):
                weight_copy(n, core, across).wait()

        @pl.when(block < 3)
        def _(block=block):
            product = jnp.dot(normed[...], weights[block], preferred_element_type=F32)
            triple[block] = (product + qkv_bias[block]).astype(BF16)

    def attend(w, carry):
        rows = pl.ds(pl.multiple_of(w * WIN, WIN), WIN)
        dead = lax.broadcasted_iota(jnp.int32, (WIN, 2 * WIN), 0) >= table[DST_WIN + w]
        zero = jnp.zeros((), BF16)
        for half in range(2):
            parts = [None] * (CHUNK // 128)
            for pair in range(HEADS // 4):
                begin = pair * 2 * HD
                low = begin // 128 * 128
                lane = low + lax.broadcasted_iota(jnp.int32, (WIN, 256), 1)
                first = (lane >= begin) & (lane < begin + HD)
                second = (lane >= begin + HD) & (lane < begin + 2 * HD)
                at = half * CHUNK + low
                q = triple[0, rows, at : at + 256]
                k = triple[1, rows, at : at + 256]
                v = triple[2, rows, at : at + 256]
                both = jnp.concatenate([jnp.where(first, q, zero), jnp.where(second, q, zero)], axis=0)
                scores = lax.dot_general(
                    k, both, (((1,), (1,)), ((), ())), preferred_element_type=F32
                )
                scores = jnp.where(dead, -1e30, scores)
                highest = jnp.max(scores, axis=0, keepdims=True)
                powers = jnp.exp2((scores - highest) * EXP2_SCALE)
                probs = powers * (1.0 / jnp.sum(powers, axis=0, keepdims=True))
                product = lax.dot_general(
                    probs.astype(BF16), v, (((0,), (0,)), ((), ())), preferred_element_type=F32
                )
                product = jnp.where(first, product[:WIN], jnp.where(second, product[WIN:], 0.0))
                for t in range(2):
                    tile, part = low // 128 + t, product[:, 128 * t : 128 * t + 128]
                    parts[tile] = part if parts[tile] is None else parts[tile] + part
            for tile in range(CHUNK // 128):
                at = half * CHUNK + tile * 128
                mixed[rows, at : at + 128] = parts[tile].astype(BF16)
        return carry

    lax.fori_loop(0, DST_WIN, attend, 0, unroll=True)

    for half in range(2):
        part = pl.ds(half * (ROWS // 2), ROWS // 2)
        encoded[part, :] = jnp.dot(mixed[part, :], weights[3], preferred_element_type=F32)
        for k in range(half * (DST_WIN // 2), (half + 1) * (DST_WIN // 2)):
            rows = pl.ds(k * WIN, WIN)
            values = windows[rows, :].astype(F32) + encoded[rows, :] + proj_bias[...]
            mean = jnp.mean(values * values, axis=-1, keepdims=True)
            alive = lax.broadcasted_iota(jnp.int32, (WIN, 1), 0) < table[DST_WIN + k]
            scale = jnp.where(alive, lax.rsqrt(mean + 1e-6), 0.0)
            values = values * scale * merge_gain[...]
            for t in range(D // 128):
                final[t, rows, :] = values[:, t * 128 : t * 128 + 128]

    at = lax.broadcasted_iota(jnp.int32, (MERGED, MERGED), 1)
    earlier = lax.broadcasted_iota(jnp.int32, (MERGED, MERGED), 0) < at
    same = owner_column[...] == owner_row[...]
    rank = jnp.sum(jnp.where(same & earlier, 1, 0), axis=0, keepdims=True)
    places = owner_row[...] * CAP + rank
    chosen = lax.broadcasted_iota(jnp.int32, (N_SEC * CAP, MERGED), 0) == places
    chosen = jnp.where(chosen, 1.0, 0.0).astype(BF16)

    def leave(p):
        cols = pl.ds(p * D, D)
        return pltpu.make_async_copy(out.at[:, cols], packed_rows.at[:, cols], psem.at[p])

    for p in range(4):
        merged = [final[t, pl.ds(p, MERGED, stride=4), :] for t in range(D // 128)]
        merged = jnp.concatenate(merged, axis=1).astype(BF16)
        packed = jnp.dot(chosen, merged, preferred_element_type=F32)
        out[:, p * D : (p + 1) * D] = packed.astype(BF16)
        leave(p).start()
    for p in range(4):
        leave(p).wait()


def encode(place, table, owner_row, owner_column, gain, qb, pb, mg, arrived, pieces):
    smem = pl.BlockSpec(memory_space=pltpu.SMEM)
    vmem = pl.BlockSpec(memory_space=pltpu.VMEM)
    hbm = pl.BlockSpec(memory_space=pl.ANY)
    return pl.pallas_call(
        encode_kernel,
        out_shape=jax.ShapeDtypeStruct((N_SEC * CAP, COLS), BF16),
        in_specs=[smem] * 2 + [vmem] * 6 + [hbm] * 17,
        out_specs=pl.BlockSpec(memory_space=pltpu.HBM),
        scratch_shapes=[
            pltpu.VMEM((N_SEC * CAP, COLS), BF16),
            pltpu.SemaphoreType.DMA((4,)),
            pltpu.VMEM((4, D, D), BF16),
            pltpu.VMEM((ROWS, D), BF16),
            pltpu.VMEM((ROWS, D), BF16),
            pltpu.VMEM((3, ROWS, D), BF16),
            pltpu.VMEM((ROWS, D), BF16),
            pltpu.VMEM((ROWS, D), F32),
            pltpu.VMEM((D // 128, ROWS, 128), F32),
            pltpu.SemaphoreType.DMA((4, 2, 2)),
            pltpu.SemaphoreType.DMA((DST_WIN,)),
        ],
        compiler_params=pltpu.CompilerParams(vmem_limit_bytes=VMEM_LIMIT),
        name="encode",
    )(place, table, owner_row, owner_column, gain, qb, pb, mg, arrived, *pieces)


def shift(n, k):
    return [(i, (i + k) % n) for i in range(n)]


SWAP = [(0, 1), (1, 0)]
CROSS = [(i, 3 - i) for i in range(4)]
CROSS3 = [(i, 7 - i) for i in range(8)]


def gather_weights(qkv_weight, proj_weight):
    y, xl, c = lax.axis_index("y"), lax.axis_index("xl"), lax.axis_index("c")
    send = lax.ppermute
    side = jnp.bitwise_xor(xl, c)
    chunk = 2 * y + side
    from_qkv = lax.dynamic_slice(qkv_weight, (0, jnp.minimum(chunk, 5) * CHUNK), (40, CHUNK))
    from_proj = lax.dynamic_slice(proj_weight, (0, jnp.maximum(chunk - 6, 0) * CHUNK), (40, CHUNK))
    own = jnp.where(chunk < 6, from_qkv, from_proj)
    column = lax.all_to_all(jnp.broadcast_to(own[None], (8, 40, CHUNK)), "z", 0, 0, tiled=True)
    return column, side


def spread_weights(column, side):
    y, xh, c = lax.axis_index("y"), lax.axis_index("xh"), lax.axis_index("c")
    send = lax.ppermute
    partner = send(column, ("xl", "c"), CROSS)
    across_column = send(column, ("xl", "xh", "c"), CROSS3)
    across_partner = send(partner, ("xl", "xh", "c"), CROSS3)

    def joined(even, odd):
        low, high = jnp.where(c == 0, even, odd), jnp.where(c == 0, odd, even)
        return jnp.concatenate([low, high], axis=1).reshape(HALF, CHUNK)

    here, across = joined(column, partner), joined(across_partner, across_column)
    up_h, down_h = send(here, "y", shift(4, 1)), send(here, "y", shift(4, -1))
    up_a, down_a = send(across, "y", shift(4, 1)), send(across, "y", shift(4, -1))
    far_h, far_a = send(up_h, "y", shift(4, 1)), send(down_a, "y", shift(4, -1))
    pieces = [here, across, up_h, up_a, down_h, down_a, far_h, far_a]
    pieces = pieces + [send(p, "c", SWAP) for p in pieces]
    return pieces, [xh, side] + [jnp.mod(y - step, 4) for step in (0, 1, -1, 2)]


def body(
    patches,
    win_count,
    dest_perm,
    win_groups,
    norm_gain,
    qkv_weight,
    qkv_bias,
    proj_weight,
    proj_bias,
    merge_gain,
    owner,
):
    position = lax.axis_index(("xh", "z", "c"))
    counts, perm = win_count[0], dest_perm[0]
    column, side = gather_weights(qkv_weight, proj_weight)
    going, table = outgoing(
        position.astype(jnp.int32).reshape(1),
        counts,
        perm,
        win_groups.reshape(N_DEV * SRC_WIN),
        patches.reshape(SRC_WIN, WIN, D),
    )
    pieces, placed = spread_weights(column, side)
    place = jnp.stack(placed).astype(jnp.int32)
    arrived = lax.all_to_all(going, ("xh", "z", "c"), split_axis=0, concat_axis=0, tiled=True)
    packed = encode(
        place,
        table,
        owner.reshape(1, MERGED),
        owner.reshape(MERGED, 1),
        norm_gain.reshape(1, D),
        qkv_bias.reshape(3, 1, D),
        proj_bias.reshape(1, D),
        merge_gain.reshape(1, D),
        arrived,
        pieces,
    )
    delivered = lax.all_to_all(packed, ("y", "xl"), split_axis=0, concat_axis=0, tiled=True)
    return delivered.reshape(1, N_SEC * CAP, COLS)


def solution(mesh):
    fine = Mesh(mesh.devices.reshape(4, 2, 2, 8, 2), ("y", "xl", "xh", "z", "c"))
    sec, dev = ("y", "xl"), ("xh", "z", "c")
    return jax.shard_map(
        body,
        mesh=fine,
        in_specs=(
            P(sec, dev, None),
            P(sec, None),
            P(sec, None),
            P(sec, None, None),
            P(),
            P(dev, None),
            P(),
            P(dev, None),
            P(),
            P(),
            P(sec, dev, None),
        ),
        out_specs=P(sec, dev, None),
        check_vma=False,
    )
```

```python
import math

import jax
import jax.numpy as jnp
from jax import lax
from jax.experimental import pallas as pl
from jax.experimental.pallas import tpu as pltpu
from jax.sharding import Mesh
from jax.sharding import PartitionSpec as P

D = 1280
HEADS = 16
HD = 80
WIN = 64
DST_WIN = 8
SRC_WIN = 24
N_DEV = 32
N_SEC = 8
CAP = 32
ROWS = DST_WIN * WIN
MERGED = ROWS // 4
COLS = 4 * D
CHUNK = 640
HALF = 640
EXP2_SCALE = HD ** (-0.5) * math.log2(math.e)
VMEM_LIMIT = 48 * 1024 * 1024

F32 = jnp.float32
BF16 = jnp.bfloat16


def slot_of(device):
    xh, z = lax.shift_right_logical(device, 4), jnp.bitwise_and(lax.shift_right_logical(device, 1), 7)
    return 4 * z + 2 * xh + jnp.bitwise_and(device, 1)


def outgoing_kernel(place, counts, perm, groups, patches, out, table, staged, in_sem, out_sem):
    pos = place[0]
    mine = counts[pos]

    def load(i):
        return pltpu.make_async_copy(patches.at[i], staged.at[i], in_sem.at[i])

    for i in range(SRC_WIN):

        @pl.when(i < mine)
        def _(i=i):
            load(i).start()

    def add(d, total):
        return total + jnp.where(d < pos, counts[d], 0)

    begin = lax.fori_loop(0, N_DEV, add, jnp.int32(0))

    def save(i):
        slot = slot_of(perm[jnp.bitwise_and(begin + i, N_DEV - 1)])
        return pltpu.make_async_copy(staged.at[i], out.at[slot], out_sem.at[i])

    for i in range(SRC_WIN):

        @pl.when(i < mine)
        def _(i=i):
            load(i).wait()
            save(i).start()

    def find(r, found):
        return jnp.where(perm[r] == pos, r, found)

    residue = lax.fori_loop(0, N_DEV, find, jnp.int32(0))

    def locate(d, before):
        count = counts[d]
        within = jnp.bitwise_and(residue - before, N_DEV - 1)

        @pl.when(within < count)
        def _():
            slot = lax.shift_right_logical(before + within, 5)
            table[slot] = slot_of(d)
            table[DST_WIN + slot] = 4 * groups[d * SRC_WIN + within]

        return before + count

    lax.fori_loop(0, N_DEV, locate, jnp.int32(0))

    for i in range(SRC_WIN):

        @pl.when(i < mine)
        def _(i=i):
            save(i).wait()


def outgoing(place, counts, perm, groups, patches):
    smem = pl.BlockSpec(memory_space=pltpu.SMEM)
    return pl.pallas_call(
        outgoing_kernel,
        out_shape=(
            jax.ShapeDtypeStruct((N_DEV, WIN, D), patches.dtype),
            jax.ShapeDtypeStruct((2 * DST_WIN,), jnp.int32),
        ),
        in_specs=[smem, smem, smem, smem, pl.BlockSpec(memory_space=pltpu.HBM)],
        out_specs=(pl.BlockSpec(memory_space=pltpu.HBM), smem),
        scratch_shapes=[
            pltpu.VMEM((SRC_WIN, WIN, D), patches.dtype),
            pltpu.SemaphoreType.DMA((SRC_WIN,)),
            pltpu.SemaphoreType.DMA((SRC_WIN,)),
        ],
        compiler_params=pltpu.CompilerParams(vmem_limit_bytes=60 * 1024 * 1024),
        name="outgoing",
    )(place, counts, perm, groups, patches)


def encode_kernel(
    place,
    table,
    owner_row,
    owner_column,
    norm_gain,
    qkv_bias,
    proj_bias,
    merge_gain,
    arrived,
    *rest,
):
    pieces = rest[:16]
    packed_rows, out, psem, weights, windows, normed, triple, mixed, encoded, final, wsem, xsem = rest[16:]
    here, side = place[0], place[1]

    def window_copy(k):
        return pltpu.make_async_copy(
            arrived.at[table[k]], windows.at[pl.ds(k * WIN, WIN)], xsem.at[k]
        )

    def weight_copy(n, core, across):
        row = jnp.bitwise_xor(here, across) * HALF
        column = jnp.bitwise_xor(side, core) * CHUNK
        to = weights.at[
            place[2 + n],
            pl.ds(pl.multiple_of(row, HALF), HALF),
            pl.ds(pl.multiple_of(column, CHUNK), CHUNK),
        ]
        return pltpu.make_async_copy(pieces[8 * core + 2 * n + across], to, wsem.at[n, core, across])

    for k in range(DST_WIN):
        window_copy(k).start()
    for n in range(4):
        for core in range(2):
            for across in range(2):
                weight_copy(n, core, across).start()
    for k in range(DST_WIN):
        window_copy(k).wait()
        rows = pl.ds(k * WIN, WIN)
        values = windows[rows, :].astype(F32)
        mean = jnp.mean(values * values, axis=-1, keepdims=True)
        normed[rows, :] = (values * lax.rsqrt(mean + 1e-6) * norm_gain[...]).astype(BF16)

    for n in range(4):
        block = place[2 + n]
        for core in range(2):
            for across in range(2):
                weight_copy(n, core, across).wait()

        @pl.when(block < 3)
        def _(block=block):
            product = jnp.dot(normed[...], weights[block], preferred_element_type=F32)
            triple[block] = (product + qkv_bias[block]).astype(BF16)

    def attend(w, carry):
        rows = pl.ds(pl.multiple_of(w * WIN, WIN), WIN)
        dead = lax.broadcasted_iota(jnp.int32, (WIN, 2 * WIN), 0) >= table[DST_WIN + w]
        zero = jnp.zeros((), BF16)
        for half in range(2):
            parts = [None] * (CHUNK // 128)
            for pair in range(HEADS // 4):
                begin = pair * 2 * HD
                low = begin // 128 * 128
                lane = low + lax.broadcasted_iota(jnp.int32, (WIN, 256), 1)
                first = (lane >= begin) & (lane < begin + HD)
                second = (lane >= begin + HD) & (lane < begin + 2 * HD)
                at = half * CHUNK + low
                q = triple[0, rows, at : at + 256]
                k = triple[1, rows, at : at + 256]
                v = triple[2, rows, at : at + 256]
                both = jnp.concatenate([jnp.where(first, q, zero), jnp.where(second, q, zero)], axis=0)
                scores = lax.dot_general(
                    k, both, (((1,), (1,)), ((), ())), preferred_element_type=F32
                )
                scores = jnp.where(dead, -1e30, scores)
                highest = jnp.max(scores, axis=0, keepdims=True)
                powers = jnp.exp2((scores - highest) * EXP2_SCALE)
                probs = powers * (1.0 / jnp.sum(powers, axis=0, keepdims=True))
                product = lax.dot_general(
                    probs.astype(BF16), v, (((0,), (0,)), ((), ())), preferred_element_type=F32
                )
                product = jnp.where(first, product[:WIN], jnp.where(second, product[WIN:], 0.0))
                for t in range(2):
                    tile, part = low // 128 + t, product[:, 128 * t : 128 * t + 128]
                    parts[tile] = part if parts[tile] is None else parts[tile] + part
            for tile in range(CHUNK // 128):
                at = half * CHUNK + tile * 128
                mixed[rows, at : at + 128] = parts[tile].astype(BF16)
        return carry

    lax.fori_loop(0, DST_WIN, attend, 0, unroll=True)

    for half in range(2):
        part = pl.ds(half * (ROWS // 2), ROWS // 2)
        encoded[part, :] = jnp.dot(mixed[part, :], weights[3], preferred_element_type=F32)
        for k in range(half * (DST_WIN // 2), (half + 1) * (DST_WIN // 2)):
            rows = pl.ds(k * WIN, WIN)
            values = windows[rows, :].astype(F32) + encoded[rows, :] + proj_bias[...]
            mean = jnp.mean(values * values, axis=-1, keepdims=True)
            alive = lax.broadcasted_iota(jnp.int32, (WIN, 1), 0) < table[DST_WIN + k]
            scale = jnp.where(alive, lax.rsqrt(mean + 1e-6), 0.0)
            values = values * scale * merge_gain[...]
            for t in range(D // 128):
                final[t, rows, :] = values[:, t * 128 : t * 128 + 128]

    at = lax.broadcasted_iota(jnp.int32, (MERGED, MERGED), 1)
    earlier = lax.broadcasted_iota(jnp.int32, (MERGED, MERGED), 0) < at
    same = owner_column[...] == owner_row[...]
    rank = jnp.sum(jnp.where(same & earlier, 1, 0), axis=0, keepdims=True)
    places = owner_row[...] * CAP + rank
    chosen = lax.broadcasted_iota(jnp.int32, (N_SEC * CAP, MERGED), 0) == places
    chosen = jnp.where(chosen, 1.0, 0.0).astype(BF16)

    def leave(p):
        cols = pl.ds(p * D, D)
        return pltpu.make_async_copy(out.at[:, cols], packed_rows.at[:, cols], psem.at[p])

    for p in range(4):
        merged = [final[t, pl.ds(p, MERGED, stride=4), :] for t in range(D // 128)]
        merged = jnp.concatenate(merged, axis=1).astype(BF16)
        packed = jnp.dot(chosen, merged, preferred_element_type=F32)
        out[:, p * D : (p + 1) * D] = packed.astype(BF16)
        leave(p).start()
    for p in range(4):
        leave(p).wait()


def encode(place, table, owner_row, owner_column, gain, qb, pb, mg, arrived, pieces):
    smem = pl.BlockSpec(memory_space=pltpu.SMEM)
    vmem = pl.BlockSpec(memory_space=pltpu.VMEM)
    hbm = pl.BlockSpec(memory_space=pl.ANY)
    return pl.pallas_call(
        encode_kernel,
        out_shape=jax.ShapeDtypeStruct((N_SEC * CAP, COLS), BF16),
        in_specs=[smem] * 2 + [vmem] * 6 + [hbm] * 17,
        out_specs=pl.BlockSpec(memory_space=pltpu.HBM),
        scratch_shapes=[
            pltpu.VMEM((N_SEC * CAP, COLS), BF16),
            pltpu.SemaphoreType.DMA((4,)),
            pltpu.VMEM((4, D, D), BF16),
            pltpu.VMEM((ROWS, D), BF16),
            pltpu.VMEM((ROWS, D), BF16),
            pltpu.VMEM((3, ROWS, D), BF16),
            pltpu.VMEM((ROWS, D), BF16),
            pltpu.VMEM((ROWS, D), F32),
            pltpu.VMEM((D // 128, ROWS, 128), F32),
            pltpu.SemaphoreType.DMA((4, 2, 2)),
            pltpu.SemaphoreType.DMA((DST_WIN,)),
        ],
        compiler_params=pltpu.CompilerParams(vmem_limit_bytes=VMEM_LIMIT),
        name="encode",
    )(place, table, owner_row, owner_column, gain, qb, pb, mg, arrived, *pieces)


def shift(n, k):
    return [(i, (i + k) % n) for i in range(n)]


SWAP = [(0, 1), (1, 0)]
CROSS = [(i, 3 - i) for i in range(4)]
CROSS3 = [(i, 7 - i) for i in range(8)]


def gather_weights(qkv_weight, proj_weight):
    y, xl, c = lax.axis_index("y"), lax.axis_index("xl"), lax.axis_index("c")
    send = lax.ppermute
    side = jnp.bitwise_xor(xl, c)
    chunk = 2 * y + side
    from_qkv = lax.dynamic_slice(qkv_weight, (0, jnp.minimum(chunk, 5) * CHUNK), (40, CHUNK))
    from_proj = lax.dynamic_slice(proj_weight, (0, jnp.maximum(chunk - 6, 0) * CHUNK), (40, CHUNK))
    own = jnp.where(chunk < 6, from_qkv, from_proj)
    column = lax.all_to_all(jnp.broadcast_to(own[None], (8, 40, CHUNK)), "z", 0, 0, tiled=True)
    return column, side


def spread_weights(column, side):
    y, xh, c = lax.axis_index("y"), lax.axis_index("xh"), lax.axis_index("c")
    send = lax.ppermute
    partner = send(column, ("xl", "c"), CROSS)
    across_column = send(column, ("xl", "xh", "c"), CROSS3)
    across_partner = send(partner, ("xl", "xh", "c"), CROSS3)

    def joined(even, odd):
        low, high = jnp.where(c == 0, even, odd), jnp.where(c == 0, odd, even)
        return jnp.concatenate([low, high], axis=1).reshape(HALF, CHUNK)

    here, across = joined(column, partner), joined(across_partner, across_column)
    up_h, down_h = send(here, "y", shift(4, 1)), send(here, "y", shift(4, -1))
    up_a, down_a = send(across, "y", shift(4, 1)), send(across, "y", shift(4, -1))
    far_h, far_a = send(up_h, "y", shift(4, 1)), send(down_a, "y", shift(4, -1))
    pieces = [here, across, up_h, up_a, down_h, down_a, far_h, far_a]
    pieces = pieces + [send(p, "c", SWAP) for p in pieces]
    return pieces, [xh, side] + [jnp.mod(y - step, 4) for step in (0, 1, -1, 2)]


def body(
    patches,
    win_count,
    dest_perm,
    win_groups,
    norm_gain,
    qkv_weight,
    qkv_bias,
    proj_weight,
    proj_bias,
    merge_gain,
    owner,
):
    position = lax.axis_index(("xh", "z", "c"))
    counts, perm = win_count[0], dest_perm[0]
    column, side = gather_weights(qkv_weight, proj_weight)
    going, table = outgoing(
        position.astype(jnp.int32).reshape(1),
        counts,
        perm,
        win_groups.reshape(N_DEV * SRC_WIN),
        patches.reshape(SRC_WIN, WIN, D),
    )
    pieces, placed = spread_weights(column, side)
    place = jnp.stack(placed).astype(jnp.int32)
    arrived = lax.all_to_all(going, ("z", "xh", "c"), split_axis=0, concat_axis=0, tiled=True)
    packed = encode(
        place,
        table,
        owner.reshape(1, MERGED),
        owner.reshape(MERGED, 1),
        norm_gain.reshape(1, D),
        qkv_bias.reshape(3, 1, D),
        proj_bias.reshape(1, D),
        merge_gain.reshape(1, D),
        arrived,
        pieces,
    )
    delivered = lax.all_to_all(packed, ("y", "xl"), split_axis=0, concat_axis=0, tiled=True)
    return delivered.reshape(1, N_SEC * CAP, COLS)


def solution(mesh):
    fine = Mesh(mesh.devices.reshape(4, 2, 2, 8, 2), ("y", "xl", "xh", "z", "c"))
    sec, dev = ("y", "xl"), ("xh", "z", "c")
    return jax.shard_map(
        body,
        mesh=fine,
        in_specs=(
            P(sec, dev, None),
            P(sec, None),
            P(sec, None),
            P(sec, None, None),
            P(),
            P(dev, None),
            P(),
            P(dev, None),
            P(),
            P(),
            P(sec, dev, None),
        ),
        out_specs=P(sec, dev, None),
        check_vma=False,
    )
```
